256 devices in a mesh: dp: 64 (over z, y, core), mp: 4 (over x).
Axes of the slice: x: 4, y: 4, z: 8, core: 2. Of those that a mesh axis runs over, the one named last changes fastest.
Arguments:
- noise_blocks: bfloat16 [512, 12800], P('dp'), may hold values from -6 to 6
- data_blocks: bfloat16 [512, 12800], P('dp'), may hold values from -6 to 6
- destination: int32 [512], replicated, may hold values from 0 to 511, as said below
- utt_blocks: int32 [64, 4], P('dp'), may hold values from 1 to 4, 8 in all within a row
- span_start: int32 [64, 4], P('dp'), may hold values from 0 to 19
- span_size: int32 [64, 4], P('dp'), may hold values from 44 to 64
- timestep: int32 [64, 4], P('dp'), may hold values from 1 to 63
- in_weight: bfloat16 [200, 1024], replicated, may hold values from -0.4375 to 0.4375
- norm_gain: bfloat16 [1024], replicated, may hold values from 0.5 to 1.5
- qkv_weight: bfloat16 [1024, 3, 512], P(None, None, 'mp'), may hold values from -4 to 4
- out_proj: bfloat16 [512, 1024], P('mp'), may hold values from -0.25 to 0.25
- final_gain: bfloat16 [1024], replicated, may hold values from 0.25 to 1.75
- vel_weight: bfloat16 [1024, 100], replicated, may hold values from -0.1875 to 0.1875
Outputs:
- grad_qkv: float32 [1024, 3, 512], P('dp', None, 'mp')
- grad_out: float32 [512, 1024], P('mp', 'dp')
The draws below stay inside these ranges and needn't reach their ends.
Inputs may be any that keep to these rules, and one draw needn't show every extreme that they name: `destination`: A permutation of the 512 bin positions; a device sends to each bin either none or exactly 1 of its blocks.
All inputs are finite; a program needn't handle non-finite values.
Results may differ from the reference program's by a relative error of at most 0.004.
Values may be sent and summed in bfloat16 or wider, within the bound.
No kernel may reach another device: no remote copies, remote signals or barrier semaphores. Data moves between devices by JAX's collectives and lax.ppermute only.
A program may use at most 64 MiB of HBM per device.

```python
import math
import jax
import jax.numpy as jnp
import numpy as np
from jax import lax

D = 1024
MEL = 100
HEAD_DIM = 64
BLOCK = 128
BLK_DEV = 8
INNER_WIDTH = 512
TOTAL_BLK = 512
CAP = 1
UTT_BIN = 4
MAXLEN = 4
N_DP = 64
N_MP = 4


def draw_destination(key, part):
    first, second, third, fourth, fifth = jax.random.split(key, 5)
    groups = BLK_DEV // CAP
    shifts = jax.random.permutation(first, N_DP)[:groups].astype(jnp.int32)
    outer = jax.random.permutation(second, N_DP).astype(jnp.int32)
    inner = jax.random.permutation(third, N_DP).astype(jnp.int32)
    source_order = jax.vmap(lambda k: jax.random.permutation(k, BLK_DEV))(jax.random.split(fourth, N_DP)).astype(jnp.int32)
    slot_order = jax.vmap(lambda k: jax.random.permutation(k, BLK_DEV))(jax.random.split(fifth, N_DP)).astype(jnp.int32)
    group = source_order // CAP
    within = source_order % CAP
    source = jnp.arange(N_DP, dtype=jnp.int32)[:, None]
    target_bin = outer[(inner[source] + shifts[group]) % N_DP]
    slot = slot_order[target_bin, group * CAP + within]
    return (target_bin * BLK_DEV + slot).reshape(-1).astype(jnp.int32)


def draw_qkv_weight(key, part):
    first = jax.random.fold_in(jax.random.fold_in(key, 11), 0)
    base = jax.random.normal(first, (D, 3, INNER_WIDTH), jnp.float32) * D ** (-0.5)
    return jnp.clip(base, -4.0, 4.0).astype(jnp.bfloat16)


def touch_ends(result, stream_key, low, largest):
    extent = result.shape
    index_at = [jax.random.randint(jax.random.fold_in(stream_key, axis), (), 0, extent[axis]) for axis in range(len(extent))]
    result = result.at[tuple(index_at)].set(low)
    longest = extent.index(max(extent))
    index_at[longest] = (index_at[longest] + 1) % extent[longest]
    return result.at[tuple(index_at)].set(largest)


def block_scale(stream_key, dims, cuts, low, high):
    level, own = 1.0, jax.random.fold_in(stream_key, 6)
    for position, shards_of in cuts:
        draws = jnp.exp(jax.random.uniform(jax.random.fold_in(own, position), (shards_of,), jnp.float32, low / len(cuts), high / len(cuts)))
        level = level * jnp.repeat(draws, dims[position] // shards_of).reshape([-1 if axis == position else 1 for axis in range(len(dims))])
    return level


def profile(amount, total, limit, skew):
    loads = [(1 << 20) // math.isqrt(grade ** skew) + 1 for grade in range(2, amount + 1)]
    spare, counts = total - limit - (amount - 1), [1] * (amount - 1)
    while spare > 0:
        movable = [i for i in range(amount - 1) if counts[i] < limit]
        pool, budget = sum([loads[i] for i in movable]), spare
        for i in movable:
            more = min(limit - counts[i], max(1, budget * loads[i] // pool), spare)
            counts[i] = counts[i] + more
            spare = spare - more
    return np.array([limit] + counts)


def ragged_sizes(own_key, number_of, total, most, slope):
    if number_of == 2:
        one = jax.random.randint(own_key, (), max(1, total - most), min(most, total - 1) + 1)
        return jnp.stack([one, total - one])
    tallies = jnp.asarray(profile(number_of, total, most, slope), jnp.int32)
    couples = (number_of - 1) // 2
    giver, sink = tallies[1:1 + 2 * couples:2], tallies[2:2 + 2 * couples:2]
    slack = jnp.minimum(giver - 1, most - sink)
    moved = jax.random.randint(jax.random.fold_in(own_key, 1), (couples,), 0, 1 << 20) % (slack + 1)
    tallies = tallies.at[1:1 + 2 * couples:2].set(giver - moved).at[2:2 + 2 * couples:2].set(sink + moved)
    return tallies[jax.random.permutation(jax.random.fold_in(own_key, 2), number_of)]


def centred(stream_key, dims, scale, limit, pieces=(), kind=jnp.bfloat16):
    entries = jax.random.normal(stream_key, dims, jnp.float32) * scale
    if len(pieces) > 0:
        entries = block_scale(stream_key, dims, pieces, -0.22, 0.18) * entries
    return jnp.clip(entries, min=-limit, max=limit).astype(kind)


def setup_inputs(seed: int = 0) -> dict:
    arg_keys = jax.random.split(jax.random.key(seed), 14)
    noise_blocks = centred(arg_keys[0], (TOTAL_BLK, BLOCK * MEL), 1.0, 6.0, ((0, 64),))
    data_blocks = centred(arg_keys[1], (TOTAL_BLK, BLOCK * MEL), 1.0, 6.0, ((0, 64),))
    destination = draw_destination(jax.random.fold_in(arg_keys[13], 71), 0)
    utt_blocks = jax.vmap(lambda own: ragged_sizes(own, UTT_BIN, BLK_DEV, MAXLEN, 2))(jax.random.split(arg_keys[3], N_DP)).reshape((N_DP, UTT_BIN)).astype(jnp.int32)
    span_start = touch_ends(jax.random.randint(arg_keys[4], (N_DP, UTT_BIN), 0, 20), jax.random.fold_in(arg_keys[4], 1), 0, 19).astype(jnp.int32)
    span_size = touch_ends(jax.random.randint(arg_keys[5], (N_DP, UTT_BIN), 44, 65), jax.random.fold_in(arg_keys[5], 1), 44, 64).astype(jnp.int32)
    timestep = touch_ends(jax.random.randint(arg_keys[6], (N_DP, UTT_BIN), 1, 64), jax.random.fold_in(arg_keys[6], 1), 1, 63).astype(jnp.int32)
    in_weight = centred(arg_keys[7], (2 * MEL, D), (2 * MEL) ** -0.5, 0.4375)
    norm_gain = jnp.clip(1.0 + 0.1 * jax.random.normal(arg_keys[8], (D,), jnp.float32), 0.5, 1.5).astype(jnp.bfloat16)
    qkv_weight = draw_qkv_weight(jax.random.fold_in(arg_keys[13], 71), 0)
    out_proj = centred(arg_keys[10], (INNER_WIDTH, D), INNER_WIDTH ** -0.5, 0.25, ((0, 4),))
    final_gain = jnp.clip(1.0 + 0.15 * jax.random.normal(arg_keys[11], (D,), jnp.float32), 0.25, 1.75).astype(jnp.bfloat16)
    vel_weight = centred(arg_keys[12], (D, MEL), D ** -0.5, 0.1875)
    return dict(noise_blocks=noise_blocks, data_blocks=data_blocks, destination=destination, utt_blocks=utt_blocks, span_start=span_start, span_size=span_size, timestep=timestep, in_weight=in_weight, norm_gain=norm_gain, qkv_weight=qkv_weight, out_proj=out_proj, final_gain=final_gain, vel_weight=vel_weight)


def frame_table(lengths, starts, sizes, steps, rows):
    lengths = lengths.astype(jnp.int32)
    ends = jnp.cumsum(lengths).astype(jnp.int32)
    frame = jnp.arange(rows, dtype=jnp.int32)
    block_index = frame // BLOCK
    segment = lax.optimization_barrier(jnp.sum((block_index[:, None] >= ends[None, :]).astype(jnp.int32), axis=1))
    member = segment[:, None] == jnp.arange(lengths.shape[0], dtype=jnp.int32)[None, :]
    first = lax.optimization_barrier(jnp.sum(jnp.where(member, (ends - lengths)[None, :], 0), axis=1)) * BLOCK
    span = lax.optimization_barrier(jnp.sum(jnp.where(member, lengths[None, :], 0), axis=1)) * BLOCK
    lower = lax.optimization_barrier(jnp.sum(jnp.where(member, starts[None, :], 0), axis=1))
    upper = lower + lax.optimization_barrier(jnp.sum(jnp.where(member, sizes[None, :], 0), axis=1))
    inside = 64 * (frame - first)
    masked = ((inside >= lower * span) & (inside < upper * span)).astype(jnp.float32)
    level = lax.optimization_barrier(jnp.sum(jnp.where(member, steps[None, :], 0), axis=1)).astype(jnp.float32) / 64.0
    return (segment, masked, level)

def attend(query, keys, values, segment):
    rows, width = query.shape
    heads = width // HEAD_DIM
    block = min(512, rows)
    reach = min(4, rows // BLOCK // 2) * BLOCK
    window = min(rows, block + 2 * reach)
    blocks = rows // block
    query_blocks = query.reshape(blocks, block, heads, HEAD_DIM)
    segment_blocks = segment.reshape(blocks, block)
    firsts = jnp.clip(jnp.arange(blocks, dtype=jnp.int32) * block - reach, 0, rows - window).astype(jnp.int32)
    keyed = keys.reshape(rows, heads, HEAD_DIM)
    valued = values.reshape(rows, heads, HEAD_DIM)

    def one_block(item):
        query_block, segment_block, first = item
        key_block = lax.dynamic_slice_in_dim(keyed, first, window, 0)
        value_block = lax.dynamic_slice_in_dim(valued, first, window, 0)
        key_segment = lax.dynamic_slice_in_dim(segment, first, window, 0)
        scores = jnp.einsum('qhd,khd->hqk', query_block, key_block, preferred_element_type=jnp.float32) * HEAD_DIM ** (-0.5)
        scores = jnp.where((segment_block[:, None] == key_segment[None, :])[None], scores, -1e+30)
        top = lax.optimization_barrier(jnp.max(scores, axis=-1, keepdims=True))
        weights = jnp.exp(scores - top)
        probs = (weights / lax.optimization_barrier(jnp.sum(weights, axis=-1, keepdims=True))).astype(jnp.bfloat16)
        return jnp.einsum('hqk,khd->qhd', probs, value_block, preferred_element_type=jnp.float32).reshape(block, width)
    return lax.map(jax.checkpoint(one_block), (query_blocks, segment_blocks, firsts)).reshape(rows, width)

def reference(noise_blocks, data_blocks, destination, utt_blocks, span_start, span_size, timestep, in_weight, norm_gain, qkv_weight, out_proj, final_gain, vel_weight):
    total = noise_blocks.shape[0]
    bins = utt_blocks.shape[0]
    per_bin = total // bins
    rows = per_bin * BLOCK
    mel = noise_blocks.shape[1] // BLOCK
    ordered_noise = jnp.zeros_like(noise_blocks).at[destination].set(noise_blocks)
    ordered_data = jnp.zeros_like(data_blocks).at[destination].set(data_blocks)
    group_width = INNER_WIDTH // N_MP
    gain_out = final_gain.astype(jnp.float32)[None, :]

    def one_bin(carry, index):
        grad_qkv, grad_out, count = carry
        noise = lax.dynamic_slice_in_dim(ordered_noise, index * per_bin, per_bin, 0).reshape(rows, mel).astype(jnp.float32)
        data = lax.dynamic_slice_in_dim(ordered_data, index * per_bin, per_bin, 0).reshape(rows, mel).astype(jnp.float32)
        lengths = lax.dynamic_index_in_dim(utt_blocks, index, 0, keepdims=False)
        starts = lax.dynamic_index_in_dim(span_start, index, 0, keepdims=False)
        sizes = lax.dynamic_index_in_dim(span_size, index, 0, keepdims=False)
        steps = lax.dynamic_index_in_dim(timestep, index, 0, keepdims=False)
        segment, masked, level = frame_table(lengths, starts, sizes, steps, rows)
        noisy = (1.0 - level[:, None]) * noise + level[:, None] * data
        cond = data * (1.0 - masked[:, None])
        target = data - noise
        inputs = jnp.concatenate([noisy, cond], axis=1).astype(jnp.bfloat16)
        hidden0 = jnp.dot(inputs, in_weight, preferred_element_type=jnp.float32)
        scale = lax.rsqrt(lax.optimization_barrier(jnp.mean(hidden0 * hidden0, axis=1, keepdims=True)) + 1e-06)
        normed = (hidden0 * scale * norm_gain.astype(jnp.float32)[None, :]).astype(jnp.bfloat16)
        query = jnp.dot(normed, qkv_weight[:, 0, :], preferred_element_type=jnp.float32).astype(jnp.bfloat16)
        keys = jnp.dot(normed, qkv_weight[:, 1, :], preferred_element_type=jnp.float32).astype(jnp.bfloat16)
        values = jnp.dot(normed, qkv_weight[:, 2, :], preferred_element_type=jnp.float32).astype(jnp.bfloat16)
        heads_out, pullback = jax.vjp(lambda a, b, c: attend(a, b, c, segment), query, keys, values)
        attended = heads_out.astype(jnp.bfloat16)
        mixed = jnp.zeros((rows, D), jnp.float32)
        for group in range(N_MP):
            lo = group * group_width
            part = jnp.dot(attended[:, lo:lo + group_width], out_proj[lo:lo + group_width, :], preferred_element_type=jnp.float32)
            mixed = mixed + part.astype(jnp.bfloat16).astype(jnp.float32)
        hidden1 = (hidden0 + mixed).astype(jnp.bfloat16)
        wide1 = lax.optimization_barrier(hidden1).astype(jnp.float32)
        rscale = lax.rsqrt(lax.optimization_barrier(jnp.mean(wide1 * wide1, axis=1, keepdims=True)) + 1e-06)
        normalized = wide1 * rscale
        final = (normalized * gain_out).astype(jnp.bfloat16)
        velocity = jnp.dot(final, vel_weight, preferred_element_type=jnp.float32)
        error = (2.0 * masked[:, None] * (velocity - target)).astype(jnp.bfloat16)
        grad_final = jnp.dot(error, vel_weight.T, preferred_element_type=jnp.float32)
        scaled = grad_final * gain_out
        back1 = (rscale * (scaled - normalized * lax.optimization_barrier(jnp.mean(scaled * normalized, axis=1, keepdims=True)))).astype(jnp.bfloat16)
        back_att = jnp.dot(back1, out_proj.T, preferred_element_type=jnp.float32).astype(jnp.bfloat16)
        dquery, dkeys, dvalues = pullback(back_att.astype(jnp.float32))
        grad_out = grad_out + jnp.dot(attended.T, back1, preferred_element_type=jnp.float32)
        terms = jnp.stack([jnp.dot(normed.T, dquery, preferred_element_type=jnp.float32), jnp.dot(normed.T, dkeys, preferred_element_type=jnp.float32), jnp.dot(normed.T, dvalues, preferred_element_type=jnp.float32)], axis=1)
        return ((grad_qkv + terms, grad_out, count + jnp.sum(masked)), None)
    start = (jnp.zeros((D, 3, INNER_WIDTH), jnp.float32), jnp.zeros((INNER_WIDTH, D), jnp.float32), jnp.zeros((), jnp.float32))
    (grad_qkv, grad_out, count), _ = lax.scan(one_bin, start, jnp.arange(bins, dtype=jnp.int32))
    return (grad_qkv / count, grad_out / count)
```

```python
import jax
import jax.numpy as jnp
from jax import lax
from jax.experimental import pallas as pl
from jax.experimental.pallas import tpu as pltpu
from jax.sharding import Mesh, PartitionSpec as P

F32, BF16 = jnp.float32, jnp.bfloat16
HEAD = 64
BLOCK = 128
MEL = 100
SLOT = 56
EPS = 1e-06
VMEM, SMEM = pltpu.VMEM, pltpu.SMEM
NT = (((1,), (1,)), ((), ()))


def vm():
    return pl.BlockSpec(memory_space=VMEM)


def sm():
    return pl.BlockSpec(memory_space=SMEM)


def params():
    return pltpu.CompilerParams(vmem_limit_bytes=48 << 20)


def dot(a, b, dims=None):
    if dims is None:
        return jnp.dot(a, b, preferred_element_type=F32)
    return lax.dot_general(a, b, dims, preferred_element_type=F32)


def pack_kernel(core, bins, own, other, out):
    c = core[0]
    for half, ref in ((0, own), (1, other)):
        out[:, half, 48:SLOT, :] = jnp.broadcast_to(ref[0, 48:SLOT, :][None], (out.shape[0], SLOT - 48, 128))
    for half, ref in ((0, own), (1, other)):
        for i in range(8):
            b = bins[half * 8 + i]

            @pl.when((b & 1) == c)
            def _():
                out[b >> 1, half] = ref[i]


def unpack_kernel(source, arrived, out, sems):
    copies = [
        pltpu.make_async_copy(arrived.at[source[j]], out.at[j], sems.at[j]) for j in range(8)
    ]
    for copy in copies:
        copy.start()
    for copy in copies:
        copy.wait()


def utterances(utt, start, size):
    first, rows = jnp.int32(0), []
    for u in range(4):
        blocks = utt[0, u]
        lo = first * BLOCK + 2 * blocks * start[0, u]
        end = (first + blocks) * BLOCK
        hi = jnp.minimum(first * BLOCK + 2 * blocks * (start[0, u] + size[0, u]), end)
        rows.append((first * BLOCK, end, lo, hi))
        first = first + blocks
    return rows


def masked_of(frame, spans):
    hit = None
    for _, _, lo, hi in spans:
        one = (frame >= lo) & (frame < hi)
        hit = one if hit is None else hit | one
    return hit


def each_utterance(utt, body):
    def step(u, first):
        blocks = utt[0, u]
        for length in range(1, 5):

            @pl.when(blocks == length)
            def _():
                body(pl.multiple_of(first * BLOCK, BLOCK), length * BLOCK)

        return first + blocks

    lax.fori_loop(0, 4, step, jnp.int32(0))


def head_mask(rows, h):
    lane = lax.broadcasted_iota(jnp.int32, (rows, 2 * HEAD), 1)
    return (lane < HEAD) if h == 0 else (lane >= HEAD)


def front_kernel(
    place, utt, start, size, level, x0, x1, x2, x3, w, gain, wqkv,
    att, inp, tgt, q, k, v, stat, vt, attt,
):
    spans = utterances(utt, start, size)
    for step, x in enumerate((x0, x1, x2, x3)):
        part = lax.rem(place[0] + step, 4)
        row = lax.broadcasted_iota(jnp.int32, (256, 128), 0)
        frame = (row >> 5) * BLOCK + part * 32 + (row & 31)
        lev = jnp.zeros((256, 128), F32)
        for u, (begin, end, _, _) in enumerate(spans):
            inside = (frame >= begin) & (frame < end)
            lev = jnp.where(inside, level[0, u].astype(F32) / 64.0, lev)
        noise, data = x[:, :128].astype(F32), x[:, 128:].astype(F32)
        noisy = (1.0 - lev) * noise + lev * data
        cond = jnp.where(masked_of(frame, spans), 0.0, data)
        both = jnp.concatenate([noisy, cond], axis=1).astype(BF16)
        diff = data - noise
        for b in range(8):
            at = pl.ds(pl.multiple_of(b * BLOCK + part * 32, 32), 32)
            inp[at, :] = both[b * 32 : b * 32 + 32]
            tgt[at, :] = diff[b * 32 : b * 32 + 32]

    def project(i, carry):
        rows = pl.ds(pl.multiple_of(i * 256, 256), 256)
        h = dot(inp[rows, :], w[...])
        scale = lax.rsqrt(jnp.mean(h * h, axis=1, keepdims=True) + EPS)
        normed = (h * scale * gain[...]).astype(BF16)
        out = dot(normed, wqkv[...])
        q[rows, :] = (out[:, :128].astype(BF16).astype(F32) * HEAD ** (-0.5)).astype(BF16)
        k[rows, :] = out[:, 128:256].astype(BF16)
        v[rows, :] = out[:, 256:].astype(BF16)
        return carry

    lax.fori_loop(0, 4, project, 0)
    vt[...] = v[...].T

    def one(first, rows):
        at = pl.ds(first, rows)
        for h in range(2):
            keys = jnp.where(head_mask(rows, h), k[at, :], jnp.zeros((), BF16))
            scores = dot(keys, q[at, :], NT)
            top = jnp.max(scores, axis=0, keepdims=True)
            weights = jnp.exp(scores - top)
            inv = 1.0 / jnp.sum(weights, axis=0, keepdims=True)
            probs = (weights * inv).astype(BF16)
            attt[h * HEAD : (h + 1) * HEAD, at] = dot(vt[h * HEAD : (h + 1) * HEAD, at], probs).astype(BF16)
            stat[h : h + 1, at] = top
            stat[h + 2 : h + 3, at] = inv

    each_utterance(utt, one)
    att[...] = attt[...].T


def back_kernel(
    place, utt, start, size, a0, a1, a2, a3, proj, inp, tgt, w, gain, fgain, vel, q, k, v, stat,
    keep, send, normed, back1, dout, kt, dqt, dk, dv, lhs,
):
    spans = utterances(utt, start, size)

    def project(i, carry):
        rows = pl.ds(pl.multiple_of(i * 256, 256), 256)
        h = dot(inp[rows, :], w[...])
        scale = lax.rsqrt(jnp.mean(h * h, axis=1, keepdims=True) + EPS)
        normed[rows, :] = (h * scale * gain[...]).astype(BF16)
        groups = jnp.concatenate([a0[rows, :], a1[rows, :], a2[rows, :], a3[rows, :]], axis=1)
        wide = (h + dot(groups, proj[...])).astype(BF16).astype(F32)
        rscale = lax.rsqrt(jnp.mean(wide * wide, axis=1, keepdims=True) + EPS)
        normalized = wide * rscale
        final = (normalized * fgain[...]).astype(BF16)
        velocity = dot(final, vel[...])
        frame = i * 256 + lax.broadcasted_iota(jnp.int32, (256, 128), 0)
        error = jnp.where(masked_of(frame, spans), 2.0 * (velocity - tgt[rows, :]), 0.0).astype(BF16)
        scaled = dot(error, vel[...], NT) * fgain[...]
        middle = jnp.mean(scaled * normalized, axis=1, keepdims=True)
        b1 = (rscale * (scaled - normalized * middle)).astype(BF16)
        back1[rows, :] = b1
        dout[rows, :] = dot(b1, proj[0:128, :], NT).astype(BF16)
        return carry

    lax.fori_loop(0, 4, project, 0)
    kt[...] = k[...].T

    def one(first, rows):
        at = pl.ds(first, rows)
        qs, ks, vs, ds = q[at, :], k[at, :], v[at, :], dout[at, :]
        dks, dvs = [], []
        for h in range(2):
            mask = head_mask(rows, h)
            zero = jnp.zeros((), BF16)
            scores = dot(jnp.where(mask, ks, zero), qs, NT)
            p = jnp.exp(scores - stat[h : h + 1, at]) * stat[h + 2 : h + 3, at]
            dp = dot(jnp.where(mask, vs, zero), ds, NT).astype(BF16).astype(F32)
            inner = jnp.sum(p * dp, axis=0, keepdims=True)
            dscore = (p * (dp - inner)).astype(BF16)
            dvs.append(dot(p.astype(BF16), ds))
            dks.append(dot(dscore, qs))
            span = slice(h * HEAD, (h + 1) * HEAD)
            dqt[span, at] = (dot(kt[span, at], dscore) * HEAD ** (-0.5)).astype(BF16)
        mask = head_mask(rows, 0)
        dk[at, :] = jnp.where(mask, dks[0], dks[1]).astype(BF16)
        dv[at, :] = jnp.where(mask, dvs[0], dvs[1]).astype(BF16)

    each_utterance(utt, one)
    lhs[0:128, :] = dqt[...]
    lhs[128:256, :] = dk[...].T
    lhs[256:384, :] = dv[...].T
    lhs[384:512, :] = a0[...].T
    mine = place[1] == 0
    for j in range(4):
        cols = slice(j * 256, (j + 1) * 256)
        top = dot(lhs[0:384, :], normed[:, cols])
        low = dot(lhs[384:512, :], back1[:, cols])
        terms = jnp.concatenate([top.T, low.T], axis=1).reshape(8, 2, 16, 512)
        even, odd = terms[:, 0], terms[:, 1]
        keep[j * 8 : j * 8 + 8] = jnp.where(mine, even, odd)
        send[j * 8 : j * 8 + 8] = jnp.where(mine, odd, even)


def shards(
    noise_blocks, data_blocks, destination, utt_blocks, span_start, span_size, timestep,
    in_weight, norm_gain, qkv_weight, out_proj, final_gain, vel_weight,
):
    z, y, c, x = (lax.axis_index(n) for n in ("z", "y", "c", "mp"))
    here = (z * 4 + y) * 2 + c
    share = noise_blocks.shape[1] // 4
    swap = [(0, 1), (1, 0)]

    def turned(a, by):
        return lax.ppermute(a, "mp", [(i, (i - by) % 4) for i in range(4)])

    bin_count = jnp.sum(2 * utt_blocks * (jnp.minimum(span_start + span_size, 64) - span_start))
    lane = lax.broadcasted_iota(jnp.int32, (8, SLOT - 50, 128), 2)
    tail = jnp.where(lane == 0, bin_count // 32, jnp.where(lane == 1, bin_count % 32, 0)).astype(BF16)
    mine = [
        lax.dynamic_slice_in_dim(a, x * share, share, 1).reshape(8, 25, 128)
        for a in (noise_blocks, data_blocks)
    ]
    own = jnp.concatenate([*mine, tail], axis=1)
    other = lax.ppermute(own, "c", swap)
    bins = destination // 8
    nearby = jnp.concatenate(
        [lax.dynamic_slice_in_dim(bins, here * 8, 8), lax.dynamic_slice_in_dim(bins, (here ^ 1) * 8, 8)]
    )
    packed = pl.pallas_call(
        pack_kernel,
        out_shape=jax.ShapeDtypeStruct((32, 2, SLOT, 128), BF16),
        in_specs=[sm(), sm(), vm(), vm()],
        out_specs=vm(),
        compiler_params=params(),
        name="pack",
    )(c[None], nearby, own, other)
    arrived = lax.all_to_all(packed, ("z", "y"), 0, 0, tiled=True).reshape(64, SLOT, 128)
    wanted = here * 8 + jnp.arange(8, dtype=jnp.int32)
    row = jnp.sum(
        jnp.where(destination[None, :] == wanted[:, None], jnp.arange(512, dtype=jnp.int32)[None, :], 0), axis=1
    )
    source = (row >> 4) * 2 + (((row >> 3) & 1) ^ c)
    blocks = pl.pallas_call(
        unpack_kernel,
        out_shape=jax.ShapeDtypeStruct((8, SLOT, 128), BF16),
        in_specs=[sm(), pl.BlockSpec(memory_space=pl.ANY)],
        out_specs=vm(),
        scratch_shapes=[pltpu.SemaphoreType.DMA((8,))],
        compiler_params=params(),
        name="unpack",
    )(source, arrived)
    counts = jnp.sum(arrived[:, 50, 0:2].astype(F32), axis=0)
    count = counts[0] * 32.0 + counts[1]
    frames = blocks[:, 0:50].reshape(8, 2, 32, MEL).transpose(0, 2, 1, 3)
    frames = jnp.pad(frames, ((0, 0), (0, 0), (0, 0), (0, 128 - MEL))).reshape(256, 256)
    pieces = [frames] + [turned(frames, by) for by in (1, 2, 3)]

    w = jnp.concatenate(
        [jnp.pad(in_weight[:MEL], ((0, 28), (0, 0))), jnp.pad(in_weight[MEL:], ((0, 28), (0, 0)))], axis=0
    )
    gain = norm_gain.astype(F32)[None, :]
    fgain = final_gain.astype(F32)[None, :]
    wqkv = qkv_weight.reshape(1024, 384)
    vel = jnp.pad(vel_weight, ((0, 0), (0, 28)))
    proj = jnp.concatenate([out_proj] + [turned(out_proj, by) for by in (1, 2, 3)], axis=0)
    place = jnp.stack([x, c])
    tables = (place, utt_blocks, span_start, span_size)

    half = jax.ShapeDtypeStruct((1024, 128), BF16)
    att, inp, tgt, q, k, v, stat = pl.pallas_call(
        front_kernel,
        out_shape=(
            half, jax.ShapeDtypeStruct((1024, 256), BF16), jax.ShapeDtypeStruct((1024, 128), F32),
            half, half, half, jax.ShapeDtypeStruct((8, 1024), F32),
        ),
        in_specs=[sm()] * 5 + [vm()] * 7,
        out_specs=(vm(),) * 7,
        scratch_shapes=[VMEM((128, 1024), BF16), VMEM((128, 1024), BF16)],
        compiler_params=params(),
        name="front",
    )(*tables, timestep, *pieces, w, gain, wqkv)
    heads = [att] + [turned(att, by) for by in (1, 2, 3)]
    terms = jax.ShapeDtypeStruct((32, 16, 512), F32)
    keep, send = pl.pallas_call(
        back_kernel,
        out_shape=(terms, terms),
        in_specs=[sm()] * 4 + [vm()] * 15,
        out_specs=(vm(), vm()),
        scratch_shapes=[
            VMEM((1024, 1024), BF16), VMEM((1024, 1024), BF16), VMEM((1024, 128), BF16),
            VMEM((128, 1024), BF16), VMEM((128, 1024), BF16), VMEM((1024, 128), BF16),
            VMEM((1024, 128), BF16), VMEM((512, 1024), BF16),
        ],
        compiler_params=params(),
        name="back",
    )(*tables, *heads, proj, inp, tgt, w, gain, fgain, vel, q, k, v, stat)
    pair = (keep + lax.ppermute(send, "c", swap)).astype(BF16)
    parts = lax.all_to_all(pair, ("z", "y"), 0, 0, tiled=True)
    total = jnp.sum(parts.astype(F32), axis=0) / count
    return (total[:, :384].reshape(16, 3, 128), total[:, 384:].T)


def solution(mesh):
    dp = ("z", "y", "c")
    fine = Mesh(mesh.devices.reshape(8, 4, 2, 4), dp + ("mp",))
    row = P(dp, None)
    in_specs = (
        row, row, P(), row, row, row, row, P(), P(), P(None, None, "mp"), P("mp", None), P(), P(),
    )
    out_specs = (P(dp, None, "mp"), P("mp", dp))
    return jax.shard_map(shards, mesh=fine, in_specs=in_specs, out_specs=out_specs, check_vma=False)
```

```python
import jax
import jax.numpy as jnp
from jax import lax
from jax.experimental import pallas as pl
from jax.experimental.pallas import tpu as pltpu
from jax.sharding import Mesh, PartitionSpec as P

F32, BF16 = jnp.float32, jnp.bfloat16
HEAD = 64
BLOCK = 128
MEL = 100
SLOT = 56
ALL = 60
EPS = 1e-06
VMEM, SMEM = pltpu.VMEM, pltpu.SMEM
NT = (((1,), (1,)), ((), ()))


def vm():
    return pl.BlockSpec(memory_space=VMEM)


def sm():
    return pl.BlockSpec(memory_space=SMEM)


def hb():
    return pl.BlockSpec(memory_space=pltpu.HBM)


def fetch(pairs, sems):
    copies = [pltpu.make_async_copy(a, b, sems.at[i]) for i, (a, b) in enumerate(pairs)]
    for copy in copies:
        copy.start()

    def wait():
        for copy in copies:
            copy.wait()

    return wait


def params(mib):
    return pltpu.CompilerParams(vmem_limit_bytes=mib << 20)


def device():
    return (lax.axis_index("z") * 4 + lax.axis_index("y")) * 2 + lax.axis_index("c")


def dot(a, b, dims=None):
    if dims is None:
        return jnp.dot(a, b, preferred_element_type=F32)
    return lax.dot_general(a, b, dims, preferred_element_type=F32)


def share_kernel(utt_hbm, start_hbm, size_hbm, noise, data, out, utt, start, size, ins, buf, sems):
    part = pl.multiple_of(lax.axis_index("mp") * 3200, 128)
    wait = fetch(
        [(utt_hbm, utt), (start_hbm, start), (size_hbm, size)]
        + [(ref.at[:, pl.ds(part, 3200)], ins.at[a]) for a, ref in enumerate((noise, data))],
        sems,
    )
    wait()
    for a in range(2):
        for r in range(25):
            buf[pl.ds(a * 25 + r, 8, stride=SLOT), :] = ins[a, :, r * 128 : (r + 1) * 128].astype(F32)
    count = jnp.int32(0)
    for u in range(4):
        count += 2 * utt[0, u] * (jnp.minimum(start[0, u] + size[0, u], 64) - start[0, u])
    lane = lax.broadcasted_iota(jnp.int32, (SLOT - 50, 128), 1)
    tail = jnp.where(lane == 0, count >> 5, jnp.where(lane == 1, count & 31, 0)).astype(F32)
    for b in range(8):
        buf[b * SLOT + 50 : (b + 1) * SLOT, :] = tail
        out[b] = buf[b * SLOT : (b + 1) * SLOT, :].astype(BF16)


def pack_kernel(bins, own, other, out, ends, tails, sem, sems):
    here = device()
    fetch([(ref.at[:, 48:SLOT, :], ends.at[half]) for half, ref in ((0, own), (1, other))], sem)()
    for half in range(2):
        tails[:, half] = jnp.broadcast_to(ends[half, 0][None], (out.shape[0], SLOT - 48, 128))
    sends = []
    for half, ref in ((0, own), (1, other)):
        for i in range(8):
            b = bins[(here ^ half) * 8 + i]
            copy = pltpu.make_async_copy(
                ref.at[i, 0:48, :], out.at[b >> 1, half, 0:48, :], sems.at[half * 8 + i]
            )
            sends.append(((b & 1) == (here & 1), copy))

            @pl.when(sends[-1][0])
            def _():
                copy.start()
                tails[b >> 1, half] = ends[half, i]

    last = pltpu.make_async_copy(tails, out.at[:, :, 48:SLOT, :], sems.at[16])
    last.start()
    for chosen, copy in sends:
        pl.when(chosen)(copy.wait)
    last.wait()


def unpack_kernel(source, arrived, out, slots, wide, rows, sems):
    fetch([(arrived.at[source[j]], slots.at[j]) for j in range(8)], sems)()
    for j in range(8):
        wide[j * SLOT : (j + 1) * SLOT, :] = slots[j].astype(F32)
    lane = lax.broadcasted_iota(jnp.int32, (8, 128), 1)
    for a in range(2):
        lines = [wide[pl.ds(a * 25 + r, 8, stride=SLOT), :] for r in range(25)]
        for f in range(32):
            r, off = divmod(f * MEL, 128)
            line = lines[r]
            if off:
                line = pltpu.roll(line, 128 - off, 1)
                if off + MEL > 128:
                    line = jnp.where(lane < 128 - off, line, pltpu.roll(lines[r + 1], 128 - off, 1))
            rows[pl.ds(f, 8, stride=32), :] = jnp.where(lane < MEL, line, 0.0)
        out[:, a * 128 : (a + 1) * 128] = rows[...].astype(BF16)


def utterances(table):
    first, rows = jnp.int32(0), []
    for u in range(4):
        blocks, start, size = (table[0, 4 * k + u] for k in range(3))
        lo = first * BLOCK + 2 * blocks * start
        end = (first + blocks) * BLOCK
        hi = jnp.minimum(first * BLOCK + 2 * blocks * (start + size), end)
        rows.append((first * BLOCK, end, lo, hi))
        first = first + blocks
    return rows


def masked_of(frame, spans):
    hit = None
    for _, _, lo, hi in spans:
        one = (frame >= lo) & (frame < hi)
        hit = one if hit is None else hit | one
    return hit


def each_utterance(table, body):
    def step(u, first):
        blocks = table[0, u]
        for length in range(1, 5):

            @pl.when(blocks == length)
            def _():
                body(pl.multiple_of(first * BLOCK, BLOCK), length * BLOCK)

        return first + blocks

    lax.fori_loop(0, 4, step, jnp.int32(0))


def head_mask(rows, h):
    lane = lax.broadcasted_iota(jnp.int32, (rows, 2 * HEAD), 1)
    return (lane < HEAD) if h == 0 else (lane >= HEAD)


def front_kernel(
    table, x0, x1, x2, x3, w, gain, wqkv,
    att, inp, tgt, q, k, v, stat, vt, attt,
):
    spans = utterances(table)
    for step, x in enumerate((x0, x1, x2, x3)):
        part = lax.rem(lax.axis_index("mp") + step, 4)
        row = lax.broadcasted_iota(jnp.int32, (256, 128), 0)
        frame = (row >> 5) * BLOCK + part * 32 + (row & 31)
        lev = jnp.zeros((256, 128), F32)
        for u, (begin, end, _, _) in enumerate(spans):
            inside = (frame >= begin) & (frame < end)
            lev = jnp.where(inside, table[0, 12 + u].astype(F32) / 64.0, lev)
        noise, data = x[:, :128].astype(F32), x[:, 128:].astype(F32)
        noisy = (1.0 - lev) * noise + lev * data
        cond = jnp.where(masked_of(frame, spans), 0.0, data)
        both = jnp.concatenate([noisy, cond], axis=1).astype(BF16)
        diff = data - noise
        for b in range(8):
            at = pl.ds(pl.multiple_of(b * BLOCK + part * 32, 32), 32)
            inp[at, :] = both[b * 32 : b * 32 + 32]
            tgt[at, :] = diff[b * 32 : b * 32 + 32]

    def project(i, carry):
        rows = pl.ds(pl.multiple_of(i * 256, 256), 256)
        h = dot(inp[rows, :], w[...])
        scale = lax.rsqrt(jnp.mean(h * h, axis=1, keepdims=True) + EPS)
        normed = (h * scale * gain[...]).astype(BF16)
        out = dot(normed, jnp.concatenate([wqkv[0], wqkv[1], wqkv[2]], axis=1))
        q[rows, :] = (out[:, :128].astype(BF16).astype(F32) * HEAD ** (-0.5)).astype(BF16)
        k[rows, :] = out[:, 128:256].astype(BF16)
        v[rows, :] = out[:, 256:].astype(BF16)
        return carry

    lax.fori_loop(0, 4, project, 0)
    vt[...] = v[...].T

    def one(first, rows):
        at = pl.ds(first, rows)
        for h in range(2):
            keys = jnp.where(head_mask(rows, h), k[at, :], jnp.zeros((), BF16))
            scores = dot(keys, q[at, :], NT)
            top = jnp.max(scores, axis=0, keepdims=True)
            weights = jnp.exp(scores - top)
            inv = 1.0 / jnp.sum(weights, axis=0, keepdims=True)
            probs = (weights * inv).astype(BF16)
            attt[h * HEAD : (h + 1) * HEAD, at] = dot(vt[h * HEAD : (h + 1) * HEAD, at], probs).astype(BF16)
            stat[h : h + 1, at] = top
            stat[h + 2 : h + 3, at] = inv

    each_utterance(table, one)
    att[...] = attt[...].T


def back_kernel(
    table, a0, a1, a2, a3, proj, inp, tgt, w, gain, fgain, vel, q, k, v, stat,
    keep, send, normed, back1, dout, kt, dqt, dk, dv, lhs,
):
    spans = utterances(table)

    def project(i, carry):
        rows = pl.ds(pl.multiple_of(i * 256, 256), 256)
        h = dot(inp[rows, :], w[...])
        scale = lax.rsqrt(jnp.mean(h * h, axis=1, keepdims=True) + EPS)
        normed[rows, :] = (h * scale * gain[...]).astype(BF16)
        groups = jnp.concatenate([a0[rows, :], a1[rows, :], a2[rows, :], a3[rows, :]], axis=1)
        wide = (h + dot(groups, proj[...])).astype(BF16).astype(F32)
        rscale = lax.rsqrt(jnp.mean(wide * wide, axis=1, keepdims=True) + EPS)
        normalized = wide * rscale
        final = (normalized * fgain[...]).astype(BF16)
        velocity = dot(final, vel[...])
        frame = i * 256 + lax.broadcasted_iota(jnp.int32, (256, 128), 0)
        error = jnp.where(masked_of(frame, spans), 2.0 * (velocity - tgt[rows, :]), 0.0).astype(BF16)
        scaled = dot(error, vel[...], NT) * fgain[...]
        middle = jnp.mean(scaled * normalized, axis=1, keepdims=True)
        b1 = (rscale * (scaled - normalized * middle)).astype(BF16)
        back1[rows, :] = b1
        dout[rows, :] = dot(b1, proj[0:128, :], NT).astype(BF16)
        return carry

    lax.fori_loop(0, 4, project, 0)
    kt[...] = k[...].T

    def one(first, rows):
        at = pl.ds(first, rows)
        qs, ks, vs, ds = q[at, :], k[at, :], v[at, :], dout[at, :]
        dks, dvs = [], []
        for h in range(2):
            mask = head_mask(rows, h)
            zero = jnp.zeros((), BF16)
            scores = dot(jnp.where(mask, ks, zero), qs, NT)
            p = jnp.exp(scores - stat[h : h + 1, at]) * stat[h + 2 : h + 3, at]
            dp = dot(jnp.where(mask, vs, zero), ds, NT).astype(BF16).astype(F32)
            inner = jnp.sum(p * dp, axis=0, keepdims=True)
            dscore = (p * (dp - inner)).astype(BF16)
            dvs.append(dot(p.astype(BF16), ds))
            dks.append(dot(dscore, qs))
            span = slice(h * HEAD, (h + 1) * HEAD)
            dqt[span, at] = (dot(kt[span, at], dscore) * HEAD ** (-0.5)).astype(BF16)
        mask = head_mask(rows, 0)
        dk[at, :] = jnp.where(mask, dks[0], dks[1]).astype(BF16)
        dv[at, :] = jnp.where(mask, dvs[0], dvs[1]).astype(BF16)

    each_utterance(table, one)
    lhs[0:128, :] = dqt[...]
    lhs[128:256, :] = dk[...].T
    lhs[256:384, :] = dv[...].T
    lhs[384:512, :] = a0[...].T
    mine = lax.axis_index("c") == 0
    for j in range(4):
        cols = slice(j * 256, (j + 1) * 256)
        top = dot(lhs[0:384, :], normed[:, cols])
        low = dot(lhs[384:512, :], back1[:, cols])
        terms = jnp.concatenate([top.T, low.T], axis=1).reshape(8, 2, 16, 512)
        even, odd = terms[:, 0], terms[:, 1]
        keep[j * 8 : j * 8 + 8] = jnp.where(mine, even, odd)
        send[j * 8 : j * 8 + 8] = jnp.where(mine, odd, even)


def finish_kernel(count, parts, qkv, out):
    total = jnp.sum(parts[...].astype(F32), axis=0) / count[...]
    for j in range(3):
        qkv[j] = total[:, j * 128 : (j + 1) * 128]
    out[...] = total[:, 384:]


def shards(
    noise_blocks, data_blocks, destination, utt_blocks, span_start, span_size, timestep,
    in_weight, norm_gain, qkv_weight, out_proj, final_gain, vel_weight,
):
    here, c = device(), lax.axis_index("c")
    swap = [(0, 1), (1, 0)]

    def turned(a, by):
        return lax.ppermute(a, "mp", [(i, (i - by) % 4) for i in range(4)])

    spans = (utt_blocks, span_start, span_size)
    own = pl.pallas_call(
        share_kernel,
        out_shape=jax.ShapeDtypeStruct((8, SLOT, 128), BF16),
        in_specs=[hb()] * 5,
        out_specs=vm(),
        scratch_shapes=[SMEM((1, 4), jnp.int32)] * 3
        + [VMEM((2, 8, 3200), BF16), VMEM((8 * SLOT, 128), F32), pltpu.SemaphoreType.DMA((5,))],
        compiler_params=params(ALL),
        name="share",
    )(*spans, noise_blocks, data_blocks)
    other = lax.ppermute(own, "c", swap)
    bins = destination // 8
    packed = pl.pallas_call(
        pack_kernel,
        out_shape=jax.ShapeDtypeStruct((32, 2, SLOT, 128), BF16),
        in_specs=[sm(), hb(), hb()],
        out_specs=hb(),
        scratch_shapes=[
            VMEM((2, 8, SLOT - 48, 128), BF16), VMEM((32, 2, SLOT - 48, 128), BF16),
            pltpu.SemaphoreType.DMA((2,)), pltpu.SemaphoreType.DMA((17,)),
        ],
        compiler_params=params(8),
        name="pack",
    )(bins, own, other)
    packed, in_weight, qkv_weight, out_proj, vel_weight, norm_gain, final_gain, table = lax.optimization_barrier(
        (packed, in_weight, qkv_weight, out_proj, vel_weight, norm_gain, final_gain, spans + (timestep,))
    )
    table = jnp.concatenate(table, axis=1)
    w = jnp.concatenate(
        [jnp.pad(in_weight[:MEL], ((0, 28), (0, 0))), jnp.pad(in_weight[MEL:], ((0, 28), (0, 0)))], axis=0
    )
    gain = norm_gain.astype(F32)[None, :]
    fgain = final_gain.astype(F32)[None, :]
    wqkv = qkv_weight.transpose(1, 0, 2)
    vel = jnp.pad(vel_weight, ((0, 0), (0, 28)))
    proj = jnp.concatenate([out_proj] + [turned(out_proj, by) for by in (1, 2, 3)], axis=0)
    arrived = lax.all_to_all(packed, ("z", "y"), 0, 0, tiled=True).reshape(64, SLOT, 128)
    wanted = here * 8 + jnp.arange(8, dtype=jnp.int32)
    row = jnp.sum(
        jnp.where(destination[None, :] == wanted[:, None], jnp.arange(512, dtype=jnp.int32)[None, :], 0), axis=1
    )
    source = (row >> 4) * 2 + (((row >> 3) & 1) ^ c)
    arrived, source, w, gain, fgain, wqkv, vel, proj, table = lax.optimization_barrier(
        (arrived, source, w, gain, fgain, wqkv, vel, proj, table)
    )
    frames = pl.pallas_call(
        unpack_kernel,
        out_shape=jax.ShapeDtypeStruct((256, 256), BF16),
        in_specs=[sm(), hb()],
        out_specs=vm(),
        scratch_shapes=[
            VMEM((8, SLOT, 128), BF16), VMEM((8 * SLOT, 128), F32), VMEM((256, 128), F32),
            pltpu.SemaphoreType.DMA((8,)),
        ],
        compiler_params=params(8),
        name="unpack",
    )(source, arrived)
    counts = jnp.sum(arrived[:, 50, 0:2].astype(F32), axis=0)
    count = counts[0] * 32.0 + counts[1]
    pieces = [frames] + [turned(frames, by) for by in (1, 2, 3)]

    half = jax.ShapeDtypeStruct((1024, 128), BF16)
    att, inp, tgt, q, k, v, stat = pl.pallas_call(
        front_kernel,
        out_shape=(
            half, jax.ShapeDtypeStruct((1024, 256), BF16), jax.ShapeDtypeStruct((1024, 128), F32),
            half, half, half, jax.ShapeDtypeStruct((8, 1024), F32),
        ),
        in_specs=[sm()] + [vm()] * 7,
        out_specs=(vm(),) * 7,
        scratch_shapes=[VMEM((128, 1024), BF16), VMEM((128, 1024), BF16)],
        compiler_params=params(20),
        name="front",
    )(table, *pieces, w, gain, wqkv)
    heads = [att] + [turned(att, by) for by in (1, 2, 3)]
    terms = jax.ShapeDtypeStruct((32, 16, 512), F32)
    keep, send = pl.pallas_call(
        back_kernel,
        out_shape=(terms, terms),
        in_specs=[sm()] + [vm()] * 15,
        out_specs=(vm(), vm()),
        scratch_shapes=[
            VMEM((1024, 1024), BF16), VMEM((1024, 1024), BF16), VMEM((1024, 128), BF16),
            VMEM((128, 1024), BF16), VMEM((128, 1024), BF16), VMEM((1024, 128), BF16),
            VMEM((1024, 128), BF16), VMEM((512, 1024), BF16),
        ],
        compiler_params=params(28),
        name="back",
    )(table, *heads, proj, inp, tgt, w, gain, fgain, vel, q, k, v, stat)
    pair = (keep + lax.ppermute(send, "c", swap)).astype(BF16)
    parts = lax.all_to_all(pair, ("z", "y"), 0, 0, tiled=True)
    grad_qkv, grad_out = pl.pallas_call(
        finish_kernel,
        out_shape=(jax.ShapeDtypeStruct((3, 16, 128), F32), jax.ShapeDtypeStruct((16, 128), F32)),
        in_specs=[vm()] * 2,
        out_specs=(vm(), vm()),
        compiler_params=params(8),
        name="finish",
    )(count.reshape(1, 1), parts)
    return (grad_qkv.transpose(1, 0, 2), grad_out.T)


def solution(mesh):
    dp = ("z", "y", "c")
    fine = Mesh(mesh.devices.reshape(8, 4, 2, 4), dp + ("mp",))
    row = P(dp, None)
    in_specs = (
        row, row, P(), row, row, row, row, P(), P(), P(None, None, "mp"), P("mp", None), P(), P(),
    )
    out_specs = (P(dp, None, "mp"), P("mp", dp))
    return jax.shard_map(shards, mesh=fine, in_specs=in_specs, out_specs=out_specs, check_vma=False)
```

```python
import jax
import jax.numpy as jnp
from jax import lax
from jax.experimental import pallas as pl
from jax.experimental.pallas import tpu as pltpu
from jax.sharding import Mesh, PartitionSpec as P

F32, BF16 = jnp.float32, jnp.bfloat16
HEAD = 64
BLOCK = 128
MEL = 100
SLOT = 56
ALL = 60
EPS = 1e-06
VMEM, SMEM = pltpu.VMEM, pltpu.SMEM
NT = (((1,), (1,)), ((), ()))


def vm():
    return pl.BlockSpec(memory_space=VMEM)


def sm():
    return pl.BlockSpec(memory_space=SMEM)


def hb():
    return pl.BlockSpec(memory_space=pltpu.HBM)


def fetch(pairs, sems):
    copies = [pltpu.make_async_copy(a, b, sems.at[i]) for i, (a, b) in enumerate(pairs)]
    for copy in copies:
        copy.start()

    def wait():
        for copy in copies:
            copy.wait()

    return wait


def params(mib):
    return pltpu.CompilerParams(vmem_limit_bytes=mib << 20)


def device():
    return (lax.axis_index("z") * 4 + lax.axis_index("y")) * 2 + lax.axis_index("c")


def dot(a, b, dims=None):
    if dims is None:
        return jnp.dot(a, b, preferred_element_type=F32)
    return lax.dot_general(a, b, dims, preferred_element_type=F32)


def share_kernel(utt_hbm, start_hbm, size_hbm, noise, data, out, utt, start, size, ins, buf, sems):
    part = pl.multiple_of(lax.axis_index("mp") * 3200, 128)
    wait = fetch(
        [(utt_hbm, utt), (start_hbm, start), (size_hbm, size)]
        + [(ref.at[:, pl.ds(part, 3200)], ins.at[a]) for a, ref in enumerate((noise, data))],
        sems,
    )
    wait()
    for a in range(2):
        for r in range(25):
            buf[pl.ds(a * 25 + r, 8, stride=SLOT), :] = ins[a, :, r * 128 : (r + 1) * 128].astype(F32)
    count = jnp.int32(0)
    for u in range(4):
        count += 2 * utt[0, u] * (jnp.minimum(start[0, u] + size[0, u], 64) - start[0, u])
    lane = lax.broadcasted_iota(jnp.int32, (SLOT - 50, 128), 1)
    tail = jnp.where(lane == 0, count >> 5, jnp.where(lane == 1, count & 31, 0)).astype(F32)
    for b in range(8):
        buf[b * SLOT + 50 : (b + 1) * SLOT, :] = tail
        out[b] = buf[b * SLOT : (b + 1) * SLOT, :].astype(BF16)


def pack_kernel(bins, own, other, out, ends, tails, sem, sems):
    here = device()
    fetch([(ref.at[:, 48:SLOT, :], ends.at[half]) for half, ref in ((0, own), (1, other))], sem)()
    for half in range(2):
        tails[:, half] = jnp.broadcast_to(ends[half, 0][None], (out.shape[0], SLOT - 48, 128))
    sends = []
    for half, ref in ((0, own), (1, other)):
        for i in range(8):
            b = bins[(here ^ half) * 8 + i]
            copy = pltpu.make_async_copy(
                ref.at[i, 0:48, :], out.at[b >> 1, half, 0:48, :], sems.at[half * 8 + i]
            )
            sends.append(((b & 1) == (here & 1), copy))

            @pl.when(sends[-1][0])
            def _():
                copy.start()
                tails[b >> 1, half] = ends[half, i]

    last = pltpu.make_async_copy(tails, out.at[:, :, 48:SLOT, :], sems.at[16])
    last.start()
    for chosen, copy in sends:
        pl.when(chosen)(copy.wait)
    last.wait()


def unpack_kernel(source, arrived, out, slots, wide, rows, sems):
    fetch([(arrived.at[source[j]], slots.at[j]) for j in range(8)], sems)()
    for j in range(8):
        wide[j * SLOT : (j + 1) * SLOT, :] = slots[j].astype(F32)
    lane = lax.broadcasted_iota(jnp.int32, (8, 128), 1)
    for a in range(2):
        lines = [wide[pl.ds(a * 25 + r, 8, stride=SLOT), :] for r in range(25)]
        for f in range(32):
            r, off = divmod(f * MEL, 128)
            line = lines[r]
            if off:
                line = pltpu.roll(line, 128 - off, 1)
                if off + MEL > 128:
                    line = jnp.where(lane < 128 - off, line, pltpu.roll(lines[r + 1], 128 - off, 1))
            rows[pl.ds(f, 8, stride=32), :] = jnp.where(lane < MEL, line, 0.0)
        out[:, a * 128 : (a + 1) * 128] = rows[...].astype(BF16)


def utterances(table):
    first, rows = jnp.int32(0), []
    for u in range(4):
        blocks, start, size = (table[0, 4 * k + u] for k in range(3))
        lo = first * BLOCK + 2 * blocks * start
        end = (first + blocks) * BLOCK
        hi = jnp.minimum(first * BLOCK + 2 * blocks * (start + size), end)
        rows.append((first * BLOCK, end, lo, hi))
        first = first + blocks
    return rows


def masked_of(frame, spans):
    hit = None
    for _, _, lo, hi in spans:
        one = (frame >= lo) & (frame < hi)
        hit = one if hit is None else hit | one
    return hit


def each_utterance(table, body):
    def step(u, first):
        blocks = table[0, u]
        for length in range(1, 5):

            @pl.when(blocks == length)
            def _():
                body(pl.multiple_of(first * BLOCK, BLOCK), length * BLOCK)

        return first + blocks

    lax.fori_loop(0, 4, step, jnp.int32(0))


def head_mask(rows, h):
    lane = lax.broadcasted_iota(jnp.int32, (rows, 2 * HEAD), 1)
    return (lane < HEAD) if h == 0 else (lane >= HEAD)


def front_kernel(
    table, x0, x1, x2, x3, w, gain, wqkv,
    att, inp, tgt, q, k, v, probs_out, vt, attt,
):
    spans = utterances(table)
    for step, x in enumerate((x0, x1, x2, x3)):
        part = lax.rem(lax.axis_index("mp") + step, 4)
        row = lax.broadcasted_iota(jnp.int32, (256, 128), 0)
        frame = (row >> 5) * BLOCK + part * 32 + (row & 31)
        lev = jnp.zeros((256, 128), F32)
        for u, (begin, end, _, _) in enumerate(spans):
            inside = (frame >= begin) & (frame < end)
            lev = jnp.where(inside, table[0, 12 + u].astype(F32) / 64.0, lev)
        noise, data = x[:, :128].astype(F32), x[:, 128:].astype(F32)
        noisy = (1.0 - lev) * noise + lev * data
        cond = jnp.where(masked_of(frame, spans), 0.0, data)
        both = jnp.concatenate([noisy, cond], axis=1).astype(BF16)
        diff = data - noise
        for b in range(8):
            at = pl.ds(pl.multiple_of(b * BLOCK + part * 32, 32), 32)
            inp[at, :] = both[b * 32 : b * 32 + 32]
            tgt[at, :] = diff[b * 32 : b * 32 + 32]

    qkv = jnp.concatenate([wqkv[0], wqkv[1], wqkv[2]], axis=1)
    for i in range(4):
        rows = pl.ds(i * 256, 256)
        h = dot(inp[rows, :], w[...])
        scale = lax.rsqrt(jnp.mean(h * h, axis=1, keepdims=True) + EPS)
        out = dot((h * scale * gain[...]).astype(BF16), qkv)
        q[rows, :] = (out[:, :128].astype(BF16).astype(F32) * HEAD ** (-0.5)).astype(BF16)
        k[rows, :] = out[:, 128:256].astype(BF16)
        v[rows, :] = out[:, 256:].astype(BF16)

    vt[...] = v[...].T

    def one(first, rows):
        at = pl.ds(first, rows)
        for h in range(2):
            keys = jnp.where(head_mask(rows, h), k[at, :], jnp.zeros((), BF16))
            scores = dot(keys, q[at, :], NT)
            top = jnp.max(scores, axis=0, keepdims=True)
            weights = jnp.exp(scores - top)
            inv = 1.0 / jnp.sum(weights, axis=0, keepdims=True)
            probs = weights * inv
            probs_out[h, at, 0:rows] = probs
            part = dot(vt[h * HEAD : (h + 1) * HEAD, at], probs.astype(BF16))
            attt[h * HEAD : (h + 1) * HEAD, at] = part.astype(BF16)

    each_utterance(table, one)
    att[...] = attt[...].T


def mid_kernel(inp, w, gain, hidden, normed):
    for i in range(4):
        rows = pl.ds(i * 256, 256)
        h = dot(inp[rows, :], w[...])
        hidden[rows, :] = h
        scale = lax.rsqrt(jnp.mean(h * h, axis=1, keepdims=True) + EPS)
        normed[rows, :] = (h * scale * gain[...]).astype(BF16)


def back_kernel(
    table, a0, a1, a2, a3, proj, hidden, normed, tgt, fgain, vel, q, k, v, probs,
    keep, send, back1, dout, kt, dqt, dk, dv, lhs,
):
    spans = utterances(table)
    for i in range(4):
        rows = pl.ds(i * 256, 256)
        groups = jnp.concatenate([a0[rows, :], a1[rows, :], a2[rows, :], a3[rows, :]], axis=1)
        wide = (hidden[rows, :] + dot(groups, proj[...])).astype(BF16).astype(F32)
        rscale = lax.rsqrt(jnp.mean(wide * wide, axis=1, keepdims=True) + EPS)
        normalized = wide * rscale
        final = (normalized * fgain[...]).astype(BF16)
        velocity = dot(final, vel[...])
        frame = i * 256 + lax.broadcasted_iota(jnp.int32, (256, 128), 0)
        error = jnp.where(masked_of(frame, spans), 2.0 * (velocity - tgt[rows, :]), 0.0).astype(BF16)
        scaled = dot(error, vel[...], NT) * fgain[...]
        middle = jnp.mean(scaled * normalized, axis=1, keepdims=True)
        b1 = (rscale * (scaled - normalized * middle)).astype(BF16)
        back1[rows, :] = b1
        dout[rows, :] = dot(b1, proj[0:128, :], NT).astype(BF16)

    kt[...] = k[...].T

    def one(first, rows):
        at = pl.ds(first, rows)
        qs, vs, ds = q[at, :], v[at, :], dout[at, :]
        dks, dvs = [], []
        for h in range(2):
            mask = head_mask(rows, h)
            zero = jnp.zeros((), BF16)
            p = probs[h, at, 0:rows]
            dp = dot(jnp.where(mask, vs, zero), ds, NT).astype(BF16).astype(F32)
            inner = jnp.sum(p * dp, axis=0, keepdims=True)
            dscore = (p * (dp - inner)).astype(BF16)
            dvs.append(dot(p.astype(BF16), ds))
            dks.append(dot(dscore, qs))
            span = slice(h * HEAD, (h + 1) * HEAD)
            dqt[span, at] = (dot(kt[span, at], dscore) * HEAD ** (-0.5)).astype(BF16)
        mask = head_mask(rows, 0)
        dk[at, :] = jnp.where(mask, dks[0], dks[1]).astype(BF16)
        dv[at, :] = jnp.where(mask, dvs[0], dvs[1]).astype(BF16)

    each_utterance(table, one)
    lhs[0:128, :] = dqt[...]
    lhs[128:256, :] = dk[...].T
    lhs[256:384, :] = dv[...].T
    lhs[384:512, :] = a0[...].T
    mine = lax.axis_index("c") == 0
    for j in range(4):
        cols = slice(j * 256, (j + 1) * 256)
        top = dot(lhs[0:384, :], normed[:, cols])
        low = dot(lhs[384:512, :], back1[:, cols])
        terms = jnp.concatenate([top.T, low.T], axis=1).reshape(8, 2, 16, 512)
        even, odd = terms[:, 0], terms[:, 1]
        keep[2 * j : 2 * j + 2] = jnp.where(mine, even, odd).reshape(2, 4, 16, 512)
        send[2 * j : 2 * j + 2] = jnp.where(mine, odd, even).reshape(2, 4, 16, 512)


def pair_kernel(keep, got, own, s1, s2, s3):
    y = lax.axis_index("y")
    own[...] = keep[:, y] + got[:, y]
    for by, ref in ((1, s1), (2, s2), (3, s3)):
        to = lax.rem(y + by, 4)
        ref[...] = (keep[:, to] + got[:, to]).astype(BF16)


def line_kernel(own, r1, r2, r3, out):
    total = own[...] + r1[...].astype(F32) + r2[...].astype(F32) + r3[...].astype(F32)
    out[...] = total.astype(BF16)


def finish_kernel(count, parts, qkv, out):
    total = jnp.sum(parts[...].astype(F32), axis=0) / count[...]
    for j in range(3):
        qkv[j] = total[:, j * 128 : (j + 1) * 128]
    out[...] = total[:, 384:]


def shards(
    noise_blocks, data_blocks, destination, utt_blocks, span_start, span_size, timestep,
    in_weight, norm_gain, qkv_weight, out_proj, final_gain, vel_weight,
):
    here, c = device(), lax.axis_index("c")
    swap = [(0, 1), (1, 0)]

    def turned(a, by):
        return lax.ppermute(a, "mp", [(i, (i - by) % 4) for i in range(4)])

    spans = (utt_blocks, span_start, span_size)
    own = pl.pallas_call(
        share_kernel,
        out_shape=jax.ShapeDtypeStruct((8, SLOT, 128), BF16),
        in_specs=[hb()] * 5,
        out_specs=vm(),
        scratch_shapes=[SMEM((1, 4), jnp.int32)] * 3
        + [VMEM((2, 8, 3200), BF16), VMEM((8 * SLOT, 128), F32), pltpu.SemaphoreType.DMA((5,))],
        compiler_params=params(ALL),
        name="share",
    )(*spans, noise_blocks, data_blocks)
    other = lax.ppermute(own, "c", swap)
    bins = destination // 8
    packed = pl.pallas_call(
        pack_kernel,
        out_shape=jax.ShapeDtypeStruct((32, 2, SLOT, 128), BF16),
        in_specs=[sm(), hb(), hb()],
        out_specs=hb(),
        scratch_shapes=[
            VMEM((2, 8, SLOT - 48, 128), BF16), VMEM((32, 2, SLOT - 48, 128), BF16),
            pltpu.SemaphoreType.DMA((2,)), pltpu.SemaphoreType.DMA((17,)),
        ],
        compiler_params=params(8),
        name="pack",
    )(bins, own, other)
    packed, in_weight, qkv_weight, out_proj, vel_weight, norm_gain, final_gain, table = lax.optimization_barrier(
        (packed, in_weight, qkv_weight, out_proj, vel_weight, norm_gain, final_gain, spans + (timestep,))
    )
    table = jnp.concatenate(table, axis=1)
    w = jnp.concatenate(
        [jnp.pad(in_weight[:MEL], ((0, 28), (0, 0))), jnp.pad(in_weight[MEL:], ((0, 28), (0, 0)))], axis=0
    )
    gain = norm_gain.astype(F32)[None, :]
    fgain = final_gain.astype(F32)[None, :]
    wqkv = qkv_weight.transpose(1, 0, 2)
    vel = jnp.pad(vel_weight, ((0, 0), (0, 28)))
    proj = jnp.concatenate([out_proj] + [turned(out_proj, by) for by in (1, 2, 3)], axis=0)
    arrived = lax.all_to_all(packed, ("z", "y"), 0, 0, tiled=True).reshape(64, SLOT, 128)
    wanted = here * 8 + jnp.arange(8, dtype=jnp.int32)
    row = jnp.sum(
        jnp.where(destination[None, :] == wanted[:, None], jnp.arange(512, dtype=jnp.int32)[None, :], 0), axis=1
    )
    source = (row >> 4) * 2 + (((row >> 3) & 1) ^ c)
    arrived, source, w, gain, fgain, wqkv, vel, proj, table = lax.optimization_barrier(
        (arrived, source, w, gain, fgain, wqkv, vel, proj, table)
    )
    frames = pl.pallas_call(
        unpack_kernel,
        out_shape=jax.ShapeDtypeStruct((256, 256), BF16),
        in_specs=[sm(), hb()],
        out_specs=vm(),
        scratch_shapes=[
            VMEM((8, SLOT, 128), BF16), VMEM((8 * SLOT, 128), F32), VMEM((256, 128), F32),
            pltpu.SemaphoreType.DMA((8,)),
        ],
        compiler_params=params(8),
        name="unpack",
    )(source, arrived)
    counts = jnp.sum(arrived[:, 50, 0:2].astype(F32), axis=0)
    count = counts[0] * 32.0 + counts[1]
    pieces = [frames] + [turned(frames, by) for by in (1, 2, 3)]

    half = jax.ShapeDtypeStruct((1024, 128), BF16)
    att, inp, tgt, q, k, v, probs = pl.pallas_call(
        front_kernel,
        out_shape=(
            half, jax.ShapeDtypeStruct((1024, 256), BF16), jax.ShapeDtypeStruct((1024, 128), F32),
            half, half, half, jax.ShapeDtypeStruct((2, 1024, 512), F32),
        ),
        in_specs=[sm()] + [vm()] * 7,
        out_specs=(vm(),) * 7,
        scratch_shapes=[VMEM((128, 1024), BF16), VMEM((128, 1024), BF16)],
        compiler_params=params(20),
        name="front",
    )(table, *pieces, w, gain, wqkv)
    hidden, normed = pl.pallas_call(
        mid_kernel,
        out_shape=(jax.ShapeDtypeStruct((1024, 1024), F32), jax.ShapeDtypeStruct((1024, 1024), BF16)),
        in_specs=[vm()] * 3,
        out_specs=(vm(),) * 2,
        compiler_params=params(14),
        cost_estimate=pl.CostEstimate(flops=1 << 29, bytes_accessed=7 << 20, transcendentals=0),
        name="mid",
    )(inp, w, gain)
    heads = [att] + [turned(att, by) for by in (1, 2, 3)]
    terms = jax.ShapeDtypeStruct((8, 4, 16, 512), F32)
    keep, send = pl.pallas_call(
        back_kernel,
        out_shape=(terms, terms),
        in_specs=[sm()] + [vm()] * 14,
        out_specs=(vm(), vm()),
        scratch_shapes=[
            VMEM((1024, 1024), BF16), VMEM((1024, 128), BF16),
            VMEM((128, 1024), BF16), VMEM((128, 1024), BF16), VMEM((1024, 128), BF16),
            VMEM((1024, 128), BF16), VMEM((512, 1024), BF16),
        ],
        compiler_params=params(28),
        name="back",
    )(table, *heads, proj, hidden, normed, tgt, fgain, vel, q, k, v, probs)
    got = lax.ppermute(send, "c", swap)
    piece = jax.ShapeDtypeStruct((8, 16, 512), BF16)
    total, *sends = pl.pallas_call(
        pair_kernel,
        out_shape=(jax.ShapeDtypeStruct((8, 16, 512), F32), piece, piece, piece),
        in_specs=[vm()] * 2,
        out_specs=(vm(),) * 4,
        compiler_params=params(8),
        name="pair",
    )(keep, got)
    others = [
        lax.ppermute(a, "y", [(i, (i + by) % 4) for i in range(4)]) for by, a in zip((1, 2, 3), sends)
    ]
    line = pl.pallas_call(
        line_kernel,
        out_shape=piece,
        in_specs=[vm()] * 4,
        out_specs=vm(),
        compiler_params=params(8),
        name="line",
    )(total, *others)
    parts = lax.all_to_all(line, "z", 0, 0, tiled=True)
    grad_qkv, grad_out = pl.pallas_call(
        finish_kernel,
        out_shape=(jax.ShapeDtypeStruct((3, 16, 128), F32), jax.ShapeDtypeStruct((16, 128), F32)),
        in_specs=[vm()] * 2,
        out_specs=(vm(), vm()),
        compiler_params=params(8),
        name="finish",
    )(count.reshape(1, 1), parts)
    return (grad_qkv.transpose(1, 0, 2), grad_out.T)


def solution(mesh):
    dp = ("z", "y", "c")
    fine = Mesh(mesh.devices.reshape(8, 4, 2, 4), dp + ("mp",))
    row = P(dp, None)
    in_specs = (
        row, row, P(), row, row, row, row, P(), P(), P(None, None, "mp"), P("mp", None), P(), P(),
    )
    out_specs = (P(dp, None, "mp"), P("mp", dp))
    return jax.shard_map(shards, mesh=fine, in_specs=in_specs, out_specs=out_specs, check_vma=False)
```

```python
import functools

import jax
import jax.numpy as jnp
from jax import lax
from jax.experimental import pallas as pl
from jax.experimental.pallas import tpu as pltpu
from jax.sharding import Mesh, PartitionSpec as P

F32, BF16 = jnp.float32, jnp.bfloat16
HEAD = 64
BLOCK = 128
MEL = 100
SLOT = 56
ALL = 60
EPS = 1e-06
VMEM, SMEM = pltpu.VMEM, pltpu.SMEM
NT = (((1,), (1,)), ((), ()))


def vm():
    return pl.BlockSpec(memory_space=VMEM)


def sm():
    return pl.BlockSpec(memory_space=SMEM)


def hb():
    return pl.BlockSpec(memory_space=pltpu.HBM)


def fetch(pairs, sems):
    copies = [pltpu.make_async_copy(a, b, sems.at[i]) for i, (a, b) in enumerate(pairs)]
    for copy in copies:
        copy.start()

    def wait():
        for copy in copies:
            copy.wait()

    return wait


def params(mib):
    return pltpu.CompilerParams(vmem_limit_bytes=int(mib * (1 << 20)))


def device():
    return (lax.axis_index("z") * 4 + lax.axis_index("y")) * 2 + lax.axis_index("c")


def dot(a, b, dims=None):
    if dims is None:
        return jnp.dot(a, b, preferred_element_type=F32)
    return lax.dot_general(a, b, dims, preferred_element_type=F32)


def share_kernel(utt_hbm, start_hbm, size_hbm, noise, data, out, utt, start, size, ins, buf, sems):
    part = pl.multiple_of(lax.axis_index("mp") * 3200, 128)
    wait = fetch(
        [(utt_hbm, utt), (start_hbm, start), (size_hbm, size)]
        + [(ref.at[:, pl.ds(part, 3200)], ins.at[a]) for a, ref in enumerate((noise, data))],
        sems,
    )
    wait()
    for a in range(2):
        for r in range(25):
            buf[pl.ds(a * 25 + r, 8, stride=SLOT), :] = ins[a, :, r * 128 : (r + 1) * 128].astype(F32)
    count = jnp.int32(0)
    for u in range(4):
        count += 2 * utt[0, u] * (jnp.minimum(start[0, u] + size[0, u], 64) - start[0, u])
    lane = lax.broadcasted_iota(jnp.int32, (SLOT - 50, 128), 1)
    tail = jnp.where(lane == 0, count >> 5, jnp.where(lane == 1, count & 31, 0)).astype(F32)
    for b in range(8):
        buf[b * SLOT + 50 : (b + 1) * SLOT, :] = tail
        out[b] = buf[b * SLOT : (b + 1) * SLOT, :].astype(BF16)


def pack_kernel(bins, own, other, out, ends, tails, sem, sems):
    here = device()
    fetch([(ref.at[:, 48:SLOT, :], ends.at[half]) for half, ref in ((0, own), (1, other))], sem)()
    for half in range(2):
        tails[:, half] = jnp.broadcast_to(ends[half, 0][None], (out.shape[0], SLOT - 48, 128))
    sends = []
    for half, ref in ((0, own), (1, other)):
        for i in range(8):
            b = bins[(here ^ half) * 8 + i]
            copy = pltpu.make_async_copy(
                ref.at[i, 0:48, :], out.at[b >> 1, half, 0:48, :], sems.at[half * 8 + i]
            )
            sends.append(((b & 1) == (here & 1), copy))

            @pl.when(sends[-1][0])
            def _():
                copy.start()
                tails[b >> 1, half] = ends[half, i]

    last = pltpu.make_async_copy(tails, out.at[:, :, 48:SLOT, :], sems.at[16])
    last.start()
    for chosen, copy in sends:
        pl.when(chosen)(copy.wait)
    last.wait()


def unpack_kernel(source, arrived, out, slots, wide, rows, sems):
    fetch([(arrived.at[source[j]], slots.at[j]) for j in range(8)], sems)()
    for j in range(8):
        wide[j * SLOT : (j + 1) * SLOT, :] = slots[j].astype(F32)
    lane = lax.broadcasted_iota(jnp.int32, (8, 128), 1)
    for a in range(2):
        lines = [wide[pl.ds(a * 25 + r, 8, stride=SLOT), :] for r in range(25)]
        for f in range(32):
            r, off = divmod(f * MEL, 128)
            line = lines[r]
            if off:
                line = pltpu.roll(line, 128 - off, 1)
                if off + MEL > 128:
                    line = jnp.where(lane < 128 - off, line, pltpu.roll(lines[r + 1], 128 - off, 1))
            rows[pl.ds(f, 8, stride=32), :] = jnp.where(lane < MEL, line, 0.0)
        out[:, a * 128 : (a + 1) * 128] = rows[...].astype(BF16)


def utterances(table):
    first, rows = jnp.int32(0), []
    for u in range(4):
        blocks, start, size = (table[0, 4 * k + u] for k in range(3))
        lo = first * BLOCK + 2 * blocks * start
        end = (first + blocks) * BLOCK
        hi = jnp.minimum(first * BLOCK + 2 * blocks * (start + size), end)
        rows.append((first * BLOCK, end, lo, hi))
        first = first + blocks
    return rows


def masked_of(frame, spans):
    hit = None
    for _, _, lo, hi in spans:
        one = (frame >= lo) & (frame < hi)
        hit = one if hit is None else hit | one
    return hit


def each_utterance(table, body):
    def step(u, first):
        blocks = table[0, u]
        for length in range(1, 5):

            @pl.when(blocks == length)
            def _():
                body(pl.multiple_of(first * BLOCK, BLOCK), length * BLOCK)

        return first + blocks

    lax.fori_loop(0, 4, step, jnp.int32(0))


def head_mask(rows, h):
    lane = lax.broadcasted_iota(jnp.int32, (rows, 2 * HEAD), 1)
    return (lane < HEAD) if h == 0 else (lane >= HEAD)


def piece_of(step, table, spans, x, w, gain, wqkv, inp, tgt):
    part = lax.rem(lax.axis_index("mp") + step, 4)
    row = lax.broadcasted_iota(jnp.int32, (256, 128), 0)
    frame = (row >> 5) * BLOCK + part * 32 + (row & 31)
    lev = jnp.zeros((256, 128), F32)
    for u, (begin, end, _, _) in enumerate(spans):
        inside = (frame >= begin) & (frame < end)
        lev = jnp.where(inside, table[0, 12 + u].astype(F32) / 64.0, lev)
    noise, data = x[:, :128].astype(F32), x[:, 128:].astype(F32)
    noisy = (1.0 - lev) * noise + lev * data
    cond = jnp.where(masked_of(frame, spans), 0.0, data)
    both = jnp.concatenate([noisy, cond], axis=1).astype(BF16)
    inp[...] = both
    tgt[...] = data - noise
    h = dot(both, w[...])
    scale = lax.rsqrt(jnp.mean(h * h, axis=1, keepdims=True) + EPS)
    weights = jnp.concatenate([wqkv[0], wqkv[1], wqkv[2]], axis=1)
    out = dot((h * scale * gain[...]).astype(BF16), weights)
    query = (out[:, 0:128].astype(BF16).astype(F32) * HEAD ** (-0.5)).astype(BF16)
    return query, out[:, 128:256].astype(BF16), out[:, 256:].astype(BF16)


def piece_kernel(step, table, x, w, gain, wqkv, inp, tgt, qkv):
    out = piece_of(step, table, utterances(table), x, w, gain, wqkv, inp, tgt)
    for j in range(3):
        qkv[:, j * 128 : (j + 1) * 128] = out[j]


def piece_rows(step):
    part = lax.rem(lax.axis_index("mp") + step, 4)
    return [(b * 32, pl.ds(pl.multiple_of(b * BLOCK + part * 32, 32), 32)) for b in range(8)]


def front_kernel(
    table, p0, p1, x2, x3, w, gain, wqkv, att, q, k, v, probs_out, i2, i3, t2, t3, vt, attt
):
    spans = utterances(table)
    late = ((2, x2, i2, t2), (3, x3, i3, t3))
    made = [piece_of(step, table, spans, x, w, gain, wqkv, i, t) for step, x, i, t in late]
    early = [[p[:, j * 128 : (j + 1) * 128] for j in range(3)] for p in (p0, p1)]
    for step, piece in enumerate(early + made):
        for r, at in piece_rows(step):
            for ref, rows in zip((q, k, v), piece):
                ref[at, :] = rows[r : r + 32]
    vt[...] = v[...].T

    def one(first, rows):
        at = pl.ds(first, rows)
        for h in range(2):
            keys = jnp.where(head_mask(rows, h), k[at, :], jnp.zeros((), BF16))
            scores = dot(keys, q[at, :], NT)
            top = jnp.max(scores, axis=0, keepdims=True)
            weights = jnp.exp(scores - top)
            inv = 1.0 / jnp.sum(weights, axis=0, keepdims=True)
            probs = weights * inv
            probs_out[h, at, 0:rows] = probs
            part = dot(vt[h * HEAD : (h + 1) * HEAD, at], probs.astype(BF16))
            attt[h * HEAD : (h + 1) * HEAD, at] = part.astype(BF16)

    each_utterance(table, one)
    att[...] = attt[...].T


def mid_kernel(i0, i1, i2, i3, t0, t1, t2, t3, w, gain, hidden, normed, tgt):
    for step, (inp, target) in enumerate(((i0, t0), (i1, t1), (i2, t2), (i3, t3))):
        h = dot(inp[...], w[...])
        scale = lax.rsqrt(jnp.mean(h * h, axis=1, keepdims=True) + EPS)
        n = (h * scale * gain[...]).astype(BF16)
        for r, at in piece_rows(step):
            hidden[at, :] = h[r : r + 32]
            normed[at, :] = n[r : r + 32]
            tgt[at, :] = target[r : r + 32, :]


def mix_kernel(hidden, a0, a3, proj, out):
    weights = jnp.concatenate([proj[0:128, :], proj[384:512, :]], axis=0)
    for i in range(4):
        rows = pl.ds(i * 256, 256)
        out[rows, :] = hidden[rows, :] + dot(jnp.concatenate([a0[rows, :], a3[rows, :]], axis=1), weights)


def back_kernel(
    table, a0, a1, a2, proj, hidden, normed, tgt, fgain, vel, q, k, v, probs,
    keep, send, back1, dout, kt, dqt, dk, dv, lhs,
):
    spans = utterances(table)
    for i in range(4):
        rows = pl.ds(i * 256, 256)
        groups = jnp.concatenate([a1[rows, :], a2[rows, :]], axis=1)
        wide = (hidden[rows, :] + dot(groups, proj[128:384, :])).astype(BF16).astype(F32)
        rscale = lax.rsqrt(jnp.mean(wide * wide, axis=1, keepdims=True) + EPS)
        normalized = wide * rscale
        final = (normalized * fgain[...]).astype(BF16)
        velocity = dot(final, vel[...])
        frame = i * 256 + lax.broadcasted_iota(jnp.int32, (256, 128), 0)
        error = jnp.where(masked_of(frame, spans), 2.0 * (velocity - tgt[rows, :]), 0.0).astype(BF16)
        scaled = dot(error, vel[...], NT) * fgain[...]
        middle = jnp.mean(scaled * normalized, axis=1, keepdims=True)
        b1 = (rscale * (scaled - normalized * middle)).astype(BF16)
        back1[rows, :] = b1
        dout[rows, :] = dot(b1, proj[0:128, :], NT).astype(BF16)

    kt[...] = k[...].T

    def one(first, rows):
        at = pl.ds(first, rows)
        qs, vs, ds = q[at, :], v[at, :], dout[at, :]
        dks, dvs = [], []
        for h in range(2):
            mask = head_mask(rows, h)
            zero = jnp.zeros((), BF16)
            p = probs[h, at, 0:rows]
            dp = dot(jnp.where(mask, vs, zero), ds, NT).astype(BF16).astype(F32)
            inner = jnp.sum(p * dp, axis=0, keepdims=True)
            dscore = (p * (dp - inner)).astype(BF16)
            dvs.append(dot(p.astype(BF16), ds))
            dks.append(dot(dscore, qs))
            span = slice(h * HEAD, (h + 1) * HEAD)
            dqt[span, at] = (dot(kt[span, at], dscore) * HEAD ** (-0.5)).astype(BF16)
        mask = head_mask(rows, 0)
        dk[at, :] = jnp.where(mask, dks[0], dks[1]).astype(BF16)
        dv[at, :] = jnp.where(mask, dvs[0], dvs[1]).astype(BF16)

    each_utterance(table, one)
    lhs[0:128, :] = dqt[...]
    lhs[128:256, :] = dk[...].T
    lhs[256:384, :] = dv[...].T
    lhs[384:512, :] = a0[...].T
    mine = lax.axis_index("c") == 0
    for j in range(4):
        cols = slice(j * 256, (j + 1) * 256)
        top = dot(lhs[0:384, :], normed[:, cols])
        low = dot(lhs[384:512, :], back1[:, cols])
        terms = jnp.concatenate([top.T, low.T], axis=1).reshape(8, 2, 16, 512)
        even, odd = terms[:, 0], terms[:, 1]
        keep[2 * j : 2 * j + 2] = jnp.where(mine, even, odd).reshape(2, 4, 16, 512)
        send[2 * j : 2 * j + 2] = jnp.where(mine, odd, even).reshape(2, 4, 16, 512).astype(BF16)


def pair_kernel(keep, got, own, s1, s2, s3):
    y = lax.axis_index("y")
    own[...] = keep[:, y] + got[:, y].astype(F32)
    for by, ref in ((1, s1), (2, s2), (3, s3)):
        to = lax.rem(y + by, 4)
        ref[...] = (keep[:, to] + got[:, to].astype(F32)).astype(BF16)


def line_kernel(own, r1, r2, r3, out):
    total = own[...] + r1[...].astype(F32) + r2[...].astype(F32) + r3[...].astype(F32)
    out[...] = total.astype(BF16)


def finish_kernel(count, parts, qkv, out):
    total = jnp.sum(parts[...].astype(F32), axis=0) / count[...]
    for j in range(3):
        qkv[j] = total[:, j * 128 : (j + 1) * 128]
    out[...] = total[:, 384:]


def shards(
    noise_blocks, data_blocks, destination, utt_blocks, span_start, span_size, timestep,
    in_weight, norm_gain, qkv_weight, out_proj, final_gain, vel_weight,
):
    here, c = device(), lax.axis_index("c")
    swap = [(0, 1), (1, 0)]

    def turned(a, by):
        return lax.ppermute(a, "mp", [(i, (i - by) % 4) for i in range(4)])

    spans = (utt_blocks, span_start, span_size)
    own = pl.pallas_call(
        share_kernel,
        out_shape=jax.ShapeDtypeStruct((8, SLOT, 128), BF16),
        in_specs=[hb()] * 5,
        out_specs=vm(),
        scratch_shapes=[SMEM((1, 4), jnp.int32)] * 3
        + [VMEM((2, 8, 3200), BF16), VMEM((8 * SLOT, 128), F32), pltpu.SemaphoreType.DMA((5,))],
        compiler_params=params(ALL),
        name="share",
    )(*spans, noise_blocks, data_blocks)
    other = lax.ppermute(own, "c", swap)
    bins = destination // 8
    packed = pl.pallas_call(
        pack_kernel,
        out_shape=jax.ShapeDtypeStruct((32, 2, SLOT, 128), BF16),
        in_specs=[sm(), hb(), hb()],
        out_specs=hb(),
        scratch_shapes=[
            VMEM((2, 8, SLOT - 48, 128), BF16), VMEM((32, 2, SLOT - 48, 128), BF16),
            pltpu.SemaphoreType.DMA((2,)), pltpu.SemaphoreType.DMA((17,)),
        ],
        compiler_params=params(8),
        name="pack",
    )(bins, own, other)
    packed, in_weight, qkv_weight, out_proj, vel_weight, norm_gain, final_gain, table = lax.optimization_barrier(
        (packed, in_weight, qkv_weight, out_proj, vel_weight, norm_gain, final_gain, spans + (timestep,))
    )
    table = jnp.concatenate(table, axis=1)
    w = jnp.concatenate(
        [jnp.pad(in_weight[:MEL], ((0, 28), (0, 0))), jnp.pad(in_weight[MEL:], ((0, 28), (0, 0)))], axis=0
    )
    gain = norm_gain.astype(F32)[None, :]
    fgain = final_gain.astype(F32)[None, :]
    wqkv = qkv_weight.transpose(1, 0, 2)
    vel = jnp.pad(vel_weight, ((0, 0), (0, 28)))
    proj = jnp.concatenate([out_proj] + [turned(out_proj, by) for by in (1, 2, 3)], axis=0)
    arrived = lax.all_to_all(packed, ("z", "y"), 0, 0, tiled=True).reshape(64, SLOT, 128)
    wanted = here * 8 + jnp.arange(8, dtype=jnp.int32)
    row = jnp.sum(
        jnp.where(destination[None, :] == wanted[:, None], jnp.arange(512, dtype=jnp.int32)[None, :], 0), axis=1
    )
    source = (row >> 4) * 2 + (((row >> 3) & 1) ^ c)
    arrived, source, w, gain, fgain, wqkv, vel, proj, table = lax.optimization_barrier(
        (arrived, source, w, gain, fgain, wqkv, vel, proj, table)
    )
    frames = pl.pallas_call(
        unpack_kernel,
        out_shape=jax.ShapeDtypeStruct((256, 256), BF16),
        in_specs=[sm(), hb()],
        out_specs=vm(),
        scratch_shapes=[
            VMEM((8, SLOT, 128), BF16), VMEM((8 * SLOT, 128), F32), VMEM((256, 128), F32),
            pltpu.SemaphoreType.DMA((8,)),
        ],
        compiler_params=params(8),
        name="unpack",
    )(source, arrived)
    counts = jnp.sum(arrived[:, 50, 0:2].astype(F32), axis=0)
    count = counts[0] * 32.0 + counts[1]
    pieces = [frames] + [turned(frames, by) for by in (1, 2, 3)]

    half = jax.ShapeDtypeStruct((1024, 128), BF16)

    def cost(flops, size):
        return pl.CostEstimate(flops=flops, bytes_accessed=size, transcendentals=0)

    def piece(step, frames):
        return pl.pallas_call(
            functools.partial(piece_kernel, step),
            out_shape=(
                jax.ShapeDtypeStruct((256, 256), BF16), jax.ShapeDtypeStruct((256, 128), F32),
                jax.ShapeDtypeStruct((256, 384), BF16),
            ),
            in_specs=[sm()] + [vm()] * 4,
            out_specs=(vm(),) * 3,
            compiler_params=params(12),
            cost_estimate=cost(1 << 29, 2 << 20),
            name=f"piece{step}",
        )(table, frames, w, gain, wqkv)

    first = [piece(step, pieces[step]) for step in (0, 1)]
    att, q, k, v, probs, *late = pl.pallas_call(
        front_kernel,
        out_shape=(half, half, half, half, jax.ShapeDtypeStruct((2, 1024, 512), F32))
        + (jax.ShapeDtypeStruct((256, 256), BF16),) * 2 + (jax.ShapeDtypeStruct((256, 128), F32),) * 2,
        in_specs=[sm()] + [vm()] * 7,
        out_specs=(vm(),) * 9,
        scratch_shapes=[VMEM((128, 1024), BF16), VMEM((128, 1024), BF16)],
        compiler_params=params(20),
        name="front",
    )(table, first[0][2], first[1][2], pieces[2], pieces[3], w, gain, wqkv)
    inp = (first[0][0], first[1][0], late[0], late[1])
    tgt = (first[0][1], first[1][1], late[2], late[3])
    heads = [att] + [turned(att, by) for by in (1, 2, 3)]
    full = jax.ShapeDtypeStruct((1024, 1024), F32)
    hidden, normed, target = pl.pallas_call(
        mid_kernel,
        out_shape=(full, jax.ShapeDtypeStruct((1024, 1024), BF16), jax.ShapeDtypeStruct((1024, 128), F32)),
        in_specs=[vm()] * 10,
        out_specs=(vm(),) * 3,
        compiler_params=params(14),
        cost_estimate=cost(1 << 29, 7 << 20),
        name="mid",
    )(*inp, *tgt, w, gain)
    hidden = pl.pallas_call(
        mix_kernel,
        out_shape=full,
        in_specs=[vm()] * 4,
        out_specs=vm(),
        input_output_aliases={0: 0},
        compiler_params=params(14),
        cost_estimate=cost(1 << 29, 7 << 20),
        name="mix",
    )(hidden, heads[0], heads[3], proj)
    keep, send = pl.pallas_call(
        back_kernel,
        out_shape=tuple(jax.ShapeDtypeStruct((8, 4, 16, 512), t) for t in (F32, BF16)),
        in_specs=[sm()] + [vm()] * 13,
        out_specs=(vm(), vm()),
        scratch_shapes=[
            VMEM((1024, 1024), BF16), VMEM((1024, 128), BF16),
            VMEM((128, 1024), BF16), VMEM((128, 1024), BF16), VMEM((1024, 128), BF16),
            VMEM((1024, 128), BF16), VMEM((512, 1024), BF16),
        ],
        compiler_params=params(28),
        name="back",
    )(table, *heads[:3], proj, hidden, normed, target, fgain, vel, q, k, v, probs)
    got = lax.ppermute(send, "c", swap)
    piece = jax.ShapeDtypeStruct((8, 16, 512), BF16)
    total, *sends = pl.pallas_call(
        pair_kernel,
        out_shape=(jax.ShapeDtypeStruct((8, 16, 512), F32), piece, piece, piece),
        in_specs=[vm()] * 2,
        out_specs=(vm(),) * 4,
        compiler_params=params(8),
        name="pair",
    )(keep, got)
    others = [
        lax.ppermute(a, "y", [(i, (i + by) % 4) for i in range(4)]) for by, a in zip((1, 2, 3), sends)
    ]
    line = pl.pallas_call(
        line_kernel,
        out_shape=piece,
        in_specs=[vm()] * 4,
        out_specs=vm(),
        compiler_params=params(8),
        name="line",
    )(total, *others)
    parts = lax.all_to_all(line, "z", 0, 0, tiled=True)
    grad_qkv, grad_out = pl.pallas_call(
        finish_kernel,
        out_shape=(jax.ShapeDtypeStruct((3, 16, 128), F32), jax.ShapeDtypeStruct((16, 128), F32)),
        in_specs=[vm()] * 2,
        out_specs=(vm(), vm()),
        compiler_params=params(8),
        name="finish",
    )(count.reshape(1, 1), parts)
    return (grad_qkv.transpose(1, 0, 2), grad_out.T)


def solution(mesh):
    dp = ("z", "y", "c")
    fine = Mesh(mesh.devices.reshape(8, 4, 2, 4), dp + ("mp",))
    row = P(dp, None)
    in_specs = (
        row, row, P(), row, row, row, row, P(), P(), P(None, None, "mp"), P("mp", None), P(), P(),
    )
    out_specs = (P(dp, None, "mp"), P("mp", dp))
    return jax.shard_map(shards, mesh=fine, in_specs=in_specs, out_specs=out_specs, check_vma=False)
```

```python
import functools

import jax
import jax.numpy as jnp
from jax import lax
from jax.experimental import pallas as pl
from jax.experimental.pallas import tpu as pltpu
from jax.sharding import Mesh, PartitionSpec as P

F32, BF16 = jnp.float32, jnp.bfloat16
HEAD = 64
BLOCK = 128
MEL = 100
SLOT = 56
ALL = 60
EPS = 1e-06
VMEM, SMEM = pltpu.VMEM, pltpu.SMEM
NT = (((1,), (1,)), ((), ()))


def vm():
    return pl.BlockSpec(memory_space=VMEM)


def sm():
    return pl.BlockSpec(memory_space=SMEM)


def hb():
    return pl.BlockSpec(memory_space=pltpu.HBM)


def fetch(pairs, sems):
    copies = [pltpu.make_async_copy(a, b, sems.at[i]) for i, (a, b) in enumerate(pairs)]
    for copy in copies:
        copy.start()

    def wait():
        for copy in copies:
            copy.wait()

    return wait


def params(mib):
    return pltpu.CompilerParams(vmem_limit_bytes=int(mib * (1 << 20)))


def device():
    return (lax.axis_index("z") * 4 + lax.axis_index("y")) * 2 + lax.axis_index("c")


def dot(a, b, dims=None):
    if dims is None:
        return jnp.dot(a, b, preferred_element_type=F32)
    return lax.dot_general(a, b, dims, preferred_element_type=F32)


def share_kernel(utt_hbm, start_hbm, size_hbm, noise, data, out, utt, start, size, ins, buf, sems):
    part = pl.multiple_of(lax.axis_index("mp") * 3200, 128)
    wait = fetch(
        [(utt_hbm, utt), (start_hbm, start), (size_hbm, size)]
        + [(ref.at[:, pl.ds(part, 3200)], ins.at[a]) for a, ref in enumerate((noise, data))],
        sems,
    )
    wait()
    for a in range(2):
        for r in range(25):
            buf[pl.ds(a * 25 + r, 8, stride=SLOT), :] = ins[a, :, r * 128 : (r + 1) * 128].astype(F32)
    count = jnp.int32(0)
    for u in range(4):
        count += 2 * utt[0, u] * (jnp.minimum(start[0, u] + size[0, u], 64) - start[0, u])
    lane = lax.broadcasted_iota(jnp.int32, (SLOT - 50, 128), 1)
    tail = jnp.where(lane == 0, count >> 5, jnp.where(lane == 1, count & 31, 0)).astype(F32)
    for b in range(8):
        buf[b * SLOT + 50 : (b + 1) * SLOT, :] = tail
        out[b] = buf[b * SLOT : (b + 1) * SLOT, :].astype(BF16)


def pack_kernel(bins, own, other, out, ends, tails, sem, sems):
    here = device()
    fetch([(ref.at[:, 48:SLOT, :], ends.at[half]) for half, ref in ((0, own), (1, other))], sem)()
    for half in range(2):
        tails[:, half] = jnp.broadcast_to(ends[half, 0][None], (out.shape[0], SLOT - 48, 128))
    sends = []
    for half, ref in ((0, own), (1, other)):
        for i in range(8):
            b = bins[(here ^ half) * 8 + i]
            copy = pltpu.make_async_copy(
                ref.at[i, 0:48, :], out.at[b >> 1, half, 0:48, :], sems.at[half * 8 + i]
            )
            sends.append(((b & 1) == (here & 1), copy))

            @pl.when(sends[-1][0])
            def _():
                copy.start()
                tails[b >> 1, half] = ends[half, i]

    last = pltpu.make_async_copy(tails, out.at[:, :, 48:SLOT, :], sems.at[16])
    last.start()
    for chosen, copy in sends:
        pl.when(chosen)(copy.wait)
    last.wait()


def unpack_kernel(source, arrived, out, slots, wide, rows, sems):
    fetch([(arrived.at[source[j]], slots.at[j]) for j in range(8)], sems)()
    for j in range(8):
        wide[j * SLOT : (j + 1) * SLOT, :] = slots[j].astype(F32)
    lane = lax.broadcasted_iota(jnp.int32, (8, 128), 1)
    for a in range(2):
        lines = [wide[pl.ds(a * 25 + r, 8, stride=SLOT), :] for r in range(25)]
        for f in range(32):
            r, off = divmod(f * MEL, 128)
            line = lines[r]
            if off:
                line = pltpu.roll(line, 128 - off, 1)
                if off + MEL > 128:
                    line = jnp.where(lane < 128 - off, line, pltpu.roll(lines[r + 1], 128 - off, 1))
            rows[pl.ds(f, 8, stride=32), :] = jnp.where(lane < MEL, line, 0.0)
        out[:, a * 128 : (a + 1) * 128] = rows[...].astype(BF16)


def utterances(table):
    first, rows = jnp.int32(0), []
    for u in range(4):
        blocks, start, size = (table[0, 4 * k + u] for k in range(3))
        lo = first * BLOCK + 2 * blocks * start
        end = (first + blocks) * BLOCK
        hi = jnp.minimum(first * BLOCK + 2 * blocks * (start + size), end)
        rows.append((first * BLOCK, end, lo, hi))
        first = first + blocks
    return rows


def masked_of(frame, spans):
    hit = None
    for _, _, lo, hi in spans:
        one = (frame >= lo) & (frame < hi)
        hit = one if hit is None else hit | one
    return hit


def each_utterance(table, body):
    def step(u, first):
        blocks = table[0, u]
        for length in range(1, 5):

            @pl.when(blocks == length)
            def _():
                body(pl.multiple_of(first * BLOCK, BLOCK), length * BLOCK)

        return first + blocks

    lax.fori_loop(0, 4, step, jnp.int32(0))


def head_mask(rows, h):
    lane = lax.broadcasted_iota(jnp.int32, (rows, 2 * HEAD), 1)
    return (lane < HEAD) if h == 0 else (lane >= HEAD)


def pieces_of(table, w, gain, wqkv, items):
    spans = utterances(table)
    made = []
    for step, x, inp, tgt in items:
        part = lax.rem(lax.axis_index("mp") + step, 4)
        row = lax.broadcasted_iota(jnp.int32, (256, 128), 0)
        frame = (row >> 5) * BLOCK + part * 32 + (row & 31)
        lev = jnp.zeros((256, 128), F32)
        for u, (begin, end, _, _) in enumerate(spans):
            inside = (frame >= begin) & (frame < end)
            lev = jnp.where(inside, table[0, 12 + u].astype(F32) / 64.0, lev)
        noise, data = x[:, :128].astype(F32), x[:, 128:].astype(F32)
        noisy = (1.0 - lev) * noise + lev * data
        cond = jnp.where(masked_of(frame, spans), 0.0, data)
        made.append(jnp.concatenate([noisy, cond], axis=1).astype(BF16))
        inp[...] = made[-1]
        tgt[...] = data - noise
    hidden = [dot(both, w[...]) for both in made]
    scales = [lax.rsqrt(jnp.mean(h * h, axis=1, keepdims=True) + EPS) for h in hidden]
    weights = jnp.concatenate([wqkv[0], wqkv[1], wqkv[2]], axis=1)
    outs = [dot((h * scale * gain[...]).astype(BF16), weights) for h, scale in zip(hidden, scales)]
    return [
        (
            (out[:, 0:128].astype(BF16).astype(F32) * HEAD ** (-0.5)).astype(BF16),
            out[:, 128:256].astype(BF16),
            out[:, 256:].astype(BF16),
        )
        for out in outs
    ]


def piece_kernel(step, table, x, w, gain, wqkv, inp, tgt, qkv):
    (out,) = pieces_of(table, w, gain, wqkv, [(step, x, inp, tgt)])
    for j in range(3):
        qkv[:, j * 128 : (j + 1) * 128] = out[j]


def piece_rows(step):
    part = lax.rem(lax.axis_index("mp") + step, 4)
    return [(b * 32, pl.ds(pl.multiple_of(b * BLOCK + part * 32, 32), 32)) for b in range(8)]


def front_kernel(
    table, p0, p1, x2, x3, w, gain, wqkv, att, attt, q, k, v, probs_out, i2, i3, t2, t3, vt
):
    made = pieces_of(table, w, gain, wqkv, [(2, x2, i2, t2), (3, x3, i3, t3)])
    early = [[p[:, j * 128 : (j + 1) * 128] for j in range(3)] for p in (p0, p1)]
    for step, piece in enumerate(early + made):
        for r, at in piece_rows(step):
            for ref, rows in zip((q, k, v), piece):
                ref[at, :] = rows[r : r + 32]
    vt[...] = v[...].T

    def one(first, rows):
        at = pl.ds(first, rows)
        keys = [jnp.where(head_mask(rows, h), k[at, :], jnp.zeros((), BF16)) for h in range(2)]
        scores = [dot(key, q[at, :], NT) for key in keys]
        weights = [jnp.exp(s - jnp.max(s, axis=0, keepdims=True)) for s in scores]
        inverse = [1.0 / jnp.sum(a, axis=0, keepdims=True) for a in weights]
        probs = [a * b for a, b in zip(weights, inverse)]
        parts = [dot(vt[h * HEAD : (h + 1) * HEAD, at], probs[h].astype(BF16)) for h in range(2)]
        for h in range(2):
            probs_out[h, at, 0:rows] = probs[h]
            attt[h * HEAD : (h + 1) * HEAD, at] = parts[h].astype(BF16)

    each_utterance(table, one)
    att[...] = attt[...].T


def mid_kernel(i0, i1, i2, i3, t0, t1, t2, t3, w, gain, k, hidden, normed, tgt, kt):
    kt[...] = k[...].T
    for step, (inp, target) in enumerate(((i0, t0), (i1, t1), (i2, t2), (i3, t3))):
        h = dot(inp[...], w[...])
        scale = lax.rsqrt(jnp.mean(h * h, axis=1, keepdims=True) + EPS)
        n = (h * scale * gain[...]).astype(BF16)
        for r, at in piece_rows(step):
            hidden[at, :] = h[r : r + 32]
            normed[at, :] = n[r : r + 32]
            tgt[at, :] = target[r : r + 32, :]


def mix_kernel(hidden, a0, a3, proj, out):
    weights = jnp.concatenate([proj[0:128, :], proj[384:512, :]], axis=0)
    for i in range(4):
        rows = pl.ds(i * 256, 256)
        out[rows, :] = hidden[rows, :] + dot(jnp.concatenate([a0[rows, :], a3[rows, :]], axis=1), weights)


def back_kernel(
    table, attt, a1, a2, proj, hidden, normed, tgt, fgain, vel, q, kt, v, probs,
    keep, send, back1, dout, dqt, dk, dv, lhs,
):
    spans = utterances(table)
    def first(i):
        rows = pl.ds(i * 256, 256)
        groups = jnp.concatenate([a1[rows, :], a2[rows, :]], axis=1)
        wide = (hidden[rows, :] + dot(groups, proj[128:384, :])).astype(BF16).astype(F32)
        return wide, lax.rsqrt(jnp.mean(wide * wide, axis=1, keepdims=True) + EPS)

    def second(i, wide, rscale):
        rows = pl.ds(i * 256, 256)
        normalized = wide * rscale
        velocity = dot((normalized * fgain[...]).astype(BF16), vel[...])
        frame = i * 256 + lax.broadcasted_iota(jnp.int32, (256, 128), 0)
        error = jnp.where(masked_of(frame, spans), 2.0 * (velocity - tgt[rows, :]), 0.0)
        return normalized, rscale, error.astype(BF16)

    def third(i, normalized, rscale, error):
        rows = pl.ds(i * 256, 256)
        scaled = dot(error, vel[...], NT) * fgain[...]
        middle = jnp.mean(scaled * normalized, axis=1, keepdims=True)
        b1 = (rscale * (scaled - normalized * middle)).astype(BF16)
        back1[rows, :] = b1
        dout[rows, :] = dot(b1, proj[0:128, :], NT).astype(BF16)

    ones = [first(i) for i in range(4)]
    twos = [second(i, *ones[i]) for i in range(4)]
    for i in range(4):
        third(i, *twos[i])


    def one(first, rows):
        at = pl.ds(first, rows)
        qs, vs, ds = q[at, :], v[at, :], dout[at, :]
        zero = jnp.zeros((), BF16)
        ps = [probs[h, at, 0:rows] for h in range(2)]
        dps = [
            dot(jnp.where(head_mask(rows, h), vs, zero), ds, NT).astype(BF16).astype(F32) for h in range(2)
        ]
        dvs = [dot(p.astype(BF16), ds) for p in ps]
        inner = [jnp.sum(p * dp, axis=0, keepdims=True) for p, dp in zip(ps, dps)]
        dscores = [(p * (dp - s)).astype(BF16) for p, dp, s in zip(ps, dps, inner)]
        dks = [dot(d, qs) for d in dscores]
        for h in range(2):
            span = slice(h * HEAD, (h + 1) * HEAD)
            dqt[span, at] = (dot(kt[span, at], dscores[h]) * HEAD ** (-0.5)).astype(BF16)
        mask = head_mask(rows, 0)
        dk[at, :] = jnp.where(mask, dks[0], dks[1]).astype(BF16)
        dv[at, :] = jnp.where(mask, dvs[0], dvs[1]).astype(BF16)

    each_utterance(table, one)
    lhs[0:128, :] = dqt[...]
    lhs[128:256, :] = dk[...].T
    lhs[256:384, :] = dv[...].T
    mine = lax.axis_index("c") == 0
    for j in range(4):
        cols = slice(j * 256, (j + 1) * 256)
        top = dot(lhs[0:384, :], normed[:, cols])
        low = dot(attt[...], back1[:, cols])
        terms = jnp.concatenate([top.T, low.T], axis=1).reshape(8, 2, 16, 512)
        even, odd = terms[:, 0], terms[:, 1]
        keep[2 * j : 2 * j + 2] = jnp.where(mine, even, odd).reshape(2, 4, 16, 512)
        send[2 * j : 2 * j + 2] = jnp.where(mine, odd, even).reshape(2, 4, 16, 512).astype(BF16)


def pair_kernel(keep, got, own, s1, s2, s3):
    y = lax.axis_index("y")
    own[...] = keep[:, y] + got[:, y].astype(F32)
    for by, ref in ((1, s1), (2, s2), (3, s3)):
        to = lax.rem(y + by, 4)
        ref[...] = (keep[:, to] + got[:, to].astype(F32)).astype(BF16)


def line_kernel(own, r1, r2, r3, out):
    total = own[...] + r1[...].astype(F32) + r2[...].astype(F32) + r3[...].astype(F32)
    out[...] = total.astype(BF16)


def finish_kernel(count, parts, qkv, out):
    total = jnp.sum(parts[...].astype(F32), axis=0) / count[...]
    for j in range(3):
        qkv[j] = total[:, j * 128 : (j + 1) * 128]
    out[...] = total[:, 384:]


def shards(
    noise_blocks, data_blocks, destination, utt_blocks, span_start, span_size, timestep,
    in_weight, norm_gain, qkv_weight, out_proj, final_gain, vel_weight,
):
    here, c = device(), lax.axis_index("c")
    swap = [(0, 1), (1, 0)]

    def turned(a, by):
        return lax.ppermute(a, "mp", [(i, (i - by) % 4) for i in range(4)])

    spans = (utt_blocks, span_start, span_size)
    own = pl.pallas_call(
        share_kernel,
        out_shape=jax.ShapeDtypeStruct((8, SLOT, 128), BF16),
        in_specs=[hb()] * 5,
        out_specs=vm(),
        scratch_shapes=[SMEM((1, 4), jnp.int32)] * 3
        + [VMEM((2, 8, 3200), BF16), VMEM((8 * SLOT, 128), F32), pltpu.SemaphoreType.DMA((5,))],
        compiler_params=params(ALL),
        name="share",
    )(*spans, noise_blocks, data_blocks)
    other = lax.ppermute(own, "c", swap)
    bins = destination // 8
    packed = pl.pallas_call(
        pack_kernel,
        out_shape=jax.ShapeDtypeStruct((32, 2, SLOT, 128), BF16),
        in_specs=[sm(), hb(), hb()],
        out_specs=hb(),
        scratch_shapes=[
            VMEM((2, 8, SLOT - 48, 128), BF16), VMEM((32, 2, SLOT - 48, 128), BF16),
            pltpu.SemaphoreType.DMA((2,)), pltpu.SemaphoreType.DMA((17,)),
        ],
        compiler_params=params(8),
        name="pack",
    )(bins, own, other)
    packed, in_weight, qkv_weight, out_proj, vel_weight, norm_gain, final_gain, table = lax.optimization_barrier(
        (packed, in_weight, qkv_weight, out_proj, vel_weight, norm_gain, final_gain, spans + (timestep,))
    )
    table = jnp.concatenate(table, axis=1)
    w = jnp.concatenate(
        [jnp.pad(in_weight[:MEL], ((0, 28), (0, 0))), jnp.pad(in_weight[MEL:], ((0, 28), (0, 0)))], axis=0
    )
    gain = norm_gain.astype(F32)[None, :]
    fgain = final_gain.astype(F32)[None, :]
    wqkv = qkv_weight.transpose(1, 0, 2)
    vel = jnp.pad(vel_weight, ((0, 0), (0, 28)))
    proj = jnp.concatenate([out_proj] + [turned(out_proj, by) for by in (1, 2, 3)], axis=0)
    arrived = lax.all_to_all(packed, ("z", "y"), 0, 0, tiled=True).reshape(64, SLOT, 128)
    wanted = here * 8 + jnp.arange(8, dtype=jnp.int32)
    row = jnp.sum(
        jnp.where(destination[None, :] == wanted[:, None], jnp.arange(512, dtype=jnp.int32)[None, :], 0), axis=1
    )
    source = (row >> 4) * 2 + (((row >> 3) & 1) ^ c)
    arrived, source, w, gain, fgain, wqkv, vel, proj, table = lax.optimization_barrier(
        (arrived, source, w, gain, fgain, wqkv, vel, proj, table)
    )
    frames = pl.pallas_call(
        unpack_kernel,
        out_shape=jax.ShapeDtypeStruct((256, 256), BF16),
        in_specs=[sm(), hb()],
        out_specs=vm(),
        scratch_shapes=[
            VMEM((8, SLOT, 128), BF16), VMEM((8 * SLOT, 128), F32), VMEM((256, 128), F32),
            pltpu.SemaphoreType.DMA((8,)),
        ],
        compiler_params=params(8),
        name="unpack",
    )(source, arrived)
    counts = jnp.sum(arrived[:, 50, 0:2].astype(F32), axis=0)
    count = counts[0] * 32.0 + counts[1]
    pieces = [frames] + [turned(frames, by) for by in (1, 2, 3)]

    half, turn = (jax.ShapeDtypeStruct(shape, BF16) for shape in ((1024, 128), (128, 1024)))

    def cost(flops, size):
        return pl.CostEstimate(flops=flops, bytes_accessed=size, transcendentals=0)

    def piece(step, frames):
        return pl.pallas_call(
            functools.partial(piece_kernel, step),
            out_shape=(
                jax.ShapeDtypeStruct((256, 256), BF16), jax.ShapeDtypeStruct((256, 128), F32),
                jax.ShapeDtypeStruct((256, 384), BF16),
            ),
            in_specs=[sm()] + [vm()] * 4,
            out_specs=(vm(),) * 3,
            compiler_params=params(12),
            cost_estimate=cost(1 << 29, 2 << 20),
            name=f"piece{step}",
        )(table, frames, w, gain, wqkv)

    first = [piece(step, pieces[step]) for step in (0, 1)]
    att, attt, q, k, v, probs, *late = pl.pallas_call(
        front_kernel,
        out_shape=(half, turn, half, half, half, jax.ShapeDtypeStruct((2, 1024, 512), F32))
        + (jax.ShapeDtypeStruct((256, 256), BF16),) * 2 + (jax.ShapeDtypeStruct((256, 128), F32),) * 2,
        in_specs=[sm()] + [vm()] * 7,
        out_specs=(vm(),) * 10,
        scratch_shapes=[VMEM((128, 1024), BF16)],
        compiler_params=params(20),
        name="front",
    )(table, first[0][2], first[1][2], pieces[2], pieces[3], w, gain, wqkv)
    inp = (first[0][0], first[1][0], late[0], late[1])
    tgt = (first[0][1], first[1][1], late[2], late[3])
    heads = [att] + [turned(att, by) for by in (1, 2, 3)]
    full = jax.ShapeDtypeStruct((1024, 1024), F32)
    hidden, normed, target, kt = pl.pallas_call(
        mid_kernel,
        out_shape=(full, jax.ShapeDtypeStruct((1024, 1024), BF16), jax.ShapeDtypeStruct((1024, 128), F32), turn),
        in_specs=[vm()] * 11,
        out_specs=(vm(),) * 4,
        compiler_params=params(14),
        cost_estimate=cost(1 << 29, 7 << 20),
        name="mid",
    )(*inp, *tgt, w, gain, k)
    hidden = pl.pallas_call(
        mix_kernel,
        out_shape=full,
        in_specs=[vm()] * 4,
        out_specs=vm(),
        input_output_aliases={0: 0},
        compiler_params=params(14),
        cost_estimate=cost(1 << 29, 7 << 20),
        name="mix",
    )(hidden, heads[0], heads[3], proj)
    keep, send = pl.pallas_call(
        back_kernel,
        out_shape=tuple(jax.ShapeDtypeStruct((8, 4, 16, 512), t) for t in (F32, BF16)),
        in_specs=[sm()] + [vm()] * 13,
        out_specs=(vm(), vm()),
        scratch_shapes=[
            VMEM((1024, 1024), BF16), VMEM((1024, 128), BF16),
            VMEM((128, 1024), BF16), VMEM((1024, 128), BF16), VMEM((1024, 128), BF16),
            VMEM((384, 1024), BF16),
        ],
        compiler_params=params(28),
        name="back",
    )(table, attt, *heads[1:3], proj, hidden, normed, target, fgain, vel, q, kt, v, probs)
    got = lax.ppermute(send, "c", swap)
    piece = jax.ShapeDtypeStruct((8, 16, 512), BF16)
    total, *sends = pl.pallas_call(
        pair_kernel,
        out_shape=(jax.ShapeDtypeStruct((8, 16, 512), F32), piece, piece, piece),
        in_specs=[vm()] * 2,
        out_specs=(vm(),) * 4,
        compiler_params=params(8),
        name="pair",
    )(keep, got)
    others = [
        lax.ppermute(a, "y", [(i, (i + by) % 4) for i in range(4)]) for by, a in zip((1, 2, 3), sends)
    ]
    line = pl.pallas_call(
        line_kernel,
        out_shape=piece,
        in_specs=[vm()] * 4,
        out_specs=vm(),
        compiler_params=params(8),
        name="line",
    )(total, *others)
    parts = lax.all_to_all(line, "z", 0, 0, tiled=True)
    grad_qkv, grad_out = pl.pallas_call(
        finish_kernel,
        out_shape=(jax.ShapeDtypeStruct((3, 16, 128), F32), jax.ShapeDtypeStruct((16, 128), F32)),
        in_specs=[vm()] * 2,
        out_specs=(vm(), vm()),
        compiler_params=params(8),
        name="finish",
    )(count.reshape(1, 1), parts)
    return (grad_qkv.transpose(1, 0, 2), grad_out.T)


def solution(mesh):
    dp = ("z", "y", "c")
    fine = Mesh(mesh.devices.reshape(8, 4, 2, 4), dp + ("mp",))
    row = P(dp, None)
    in_specs = (
        row, row, P(), row, row, row, row, P(), P(), P(None, None, "mp"), P("mp", None), P(), P(),
    )
    out_specs = (P(dp, None, "mp"), P("mp", dp))
    return jax.shard_map(shards, mesh=fine, in_specs=in_specs, out_specs=out_specs, check_vma=False)
```

```python
import functools

import jax
import jax.numpy as jnp
from jax import lax
from jax.experimental import pallas as pl
from jax.experimental.pallas import tpu as pltpu
from jax.sharding import Mesh, PartitionSpec as P

F32, BF16 = jnp.float32, jnp.bfloat16
HEAD = 64
BLOCK = 128
MEL = 100
SLOT = 56
PAIR = 104
ALL = 60
EPS = 1e-06
VMEM, SMEM = pltpu.VMEM, pltpu.SMEM
NT = (((1,), (1,)), ((), ()))


def vm():
    return pl.BlockSpec(memory_space=VMEM)


def sm():
    return pl.BlockSpec(memory_space=SMEM)


def hb():
    return pl.BlockSpec(memory_space=pltpu.HBM)


def fetch(pairs, sems):
    copies = [pltpu.make_async_copy(a, b, sems.at[i]) for i, (a, b) in enumerate(pairs)]
    for copy in copies:
        copy.start()

    def wait():
        for copy in copies:
            copy.wait()

    return wait


def params(mib):
    return pltpu.CompilerParams(vmem_limit_bytes=int(mib * (1 << 20)))


def device():
    return (lax.axis_index("z") * 4 + lax.axis_index("y")) * 2 + lax.axis_index("c")


def dot(a, b, dims=None):
    if dims is None:
        return jnp.dot(a, b, preferred_element_type=F32)
    return lax.dot_general(a, b, dims, preferred_element_type=F32)


def share_kernel(utt_hbm, start_hbm, size_hbm, noise, data, out, utt, start, size, ins, buf, sems):
    part = pl.multiple_of(lax.axis_index("mp") * 3200, 128)
    wait = fetch(
        [(utt_hbm, utt), (start_hbm, start), (size_hbm, size)]
        + [(ref.at[:, pl.ds(part, 3200)], ins.at[a]) for a, ref in enumerate((noise, data))],
        sems,
    )
    wait()
    for a in range(2):
        for r in range(25):
            buf[pl.ds(a * 25 + r, 8, stride=SLOT), :] = ins[a, :, r * 128 : (r + 1) * 128].astype(F32)
    count = jnp.int32(0)
    for u in range(4):
        count += 2 * utt[0, u] * (jnp.minimum(start[0, u] + size[0, u], 64) - start[0, u])
    lane = lax.broadcasted_iota(jnp.int32, (SLOT - 52, 128), 1)
    tail = jnp.where(lane == 0, count >> 5, jnp.where(lane == 1, count & 31, 0)).astype(F32)
    for b in range(8):
        buf[b * SLOT + 50 : b * SLOT + 52, :] = buf[b * SLOT + 48 : b * SLOT + 50, :]
        buf[b * SLOT + 52 : (b + 1) * SLOT, :] = tail
        out[b] = buf[b * SLOT : (b + 1) * SLOT, :].astype(BF16)


def pack_kernel(bins, own, other, out, ends, wide, tails, sem, sems):
    here = device()
    fetch([(ref.at[:, 48:SLOT, :], ends.at[half]) for half, ref in ((0, own), (1, other))], sem)()
    row = lax.broadcasted_iota(jnp.int32, (8, 128), 0)
    counts = jnp.where(row == 4, ends[0, 0].astype(F32), ends[1, 0].astype(F32))
    wide[...] = jnp.broadcast_to(counts[None], wide.shape)
    sends = []
    for half, ref in ((0, own), (1, other)):
        for i in range(8):
            b = bins[(here ^ half) * 8 + i]
            copy = pltpu.make_async_copy(
                ref.at[i, 0:48, :], out.at[b >> 1, half * 48 : half * 48 + 48, :], sems.at[half * 8 + i]
            )
            sends.append(((b & 1) == (here & 1), copy))

            @pl.when(sends[-1][0])
            def _():
                copy.start()
                mine = (row >> 1) == half
                wide[b >> 1] = jnp.where(mine, ends[half, i].astype(F32), wide[b >> 1])

    tails[...] = wide[...].astype(BF16)
    last = pltpu.make_async_copy(tails, out.at[:, 96:PAIR, :], sems.at[16])
    last.start()
    for chosen, copy in sends:
        pl.when(chosen)(copy.wait)
    last.wait()


def unpack_kernel(source, arrived, out, slots, ends, wide, rows, sems):
    pairs = []
    for j in range(8):
        chip, half = source[j] >> 1, source[j] & 1
        body = arrived.at[chip, pl.ds(pl.multiple_of(half * 48, 16), 48), :]
        pairs += [(body, slots.at[j, 0:48, :]), (arrived.at[chip, 96:PAIR, :], ends.at[j])]
    fetch(pairs, sems)()
    for j in range(8):
        wide[j * SLOT : j * SLOT + 48, :] = slots[j].astype(F32)
        end = ends[j].astype(F32)
        wide[j * SLOT + 48 : j * SLOT + 50, :] = jnp.where((source[j] & 1) == 0, end[0:2], end[2:4])
    lane = lax.broadcasted_iota(jnp.int32, (8, 128), 1)
    for a in range(2):
        lines = [wide[pl.ds(a * 25 + r, 8, stride=SLOT), :] for r in range(25)]
        for f in range(32):
            r, off = divmod(f * MEL, 128)
            line = lines[r]
            if off:
                line = pltpu.roll(line, 128 - off, 1)
                if off + MEL > 128:
                    line = jnp.where(lane < 128 - off, line, pltpu.roll(lines[r + 1], 128 - off, 1))
            rows[pl.ds(f, 8, stride=32), :] = jnp.where(lane < MEL, line, 0.0)
        out[:, a * 128 : (a + 1) * 128] = rows[...].astype(BF16)


def utterances(table):
    first, rows = jnp.int32(0), []
    for u in range(4):
        blocks, start, size = (table[0, 4 * k + u] for k in range(3))
        lo = first * BLOCK + 2 * blocks * start
        end = (first + blocks) * BLOCK
        hi = jnp.minimum(first * BLOCK + 2 * blocks * (start + size), end)
        rows.append((first * BLOCK, end, lo, hi))
        first = first + blocks
    return rows


def masked_of(frame, spans):
    hit = None
    for _, _, lo, hi in spans:
        one = (frame >= lo) & (frame < hi)
        hit = one if hit is None else hit | one
    return hit


def each_utterance(table, body):
    def step(u, first):
        blocks = table[0, u]
        for length in range(1, 5):

            @pl.when(blocks == length)
            def _():
                body(pl.multiple_of(first * BLOCK, BLOCK), length * BLOCK)

        return first + blocks

    lax.fori_loop(0, 4, step, jnp.int32(0))


def head_mask(rows, h):
    lane = lax.broadcasted_iota(jnp.int32, (rows, 2 * HEAD), 1)
    return (lane < HEAD) if h == 0 else (lane >= HEAD)


def pieces_of(table, w, gain, wqkv, items):
    spans = utterances(table)
    made = []
    for step, x, inp, tgt in items:
        part = lax.rem(lax.axis_index("mp") + step, 4)
        row = lax.broadcasted_iota(jnp.int32, (256, 128), 0)
        frame = (row >> 5) * BLOCK + part * 32 + (row & 31)
        lev = jnp.zeros((256, 128), F32)
        for u, (begin, end, _, _) in enumerate(spans):
            inside = (frame >= begin) & (frame < end)
            lev = jnp.where(inside, table[0, 12 + u].astype(F32) / 64.0, lev)
        noise, data = x[:, :128].astype(F32), x[:, 128:].astype(F32)
        noisy = (1.0 - lev) * noise + lev * data
        cond = jnp.where(masked_of(frame, spans), 0.0, data)
        made.append(jnp.concatenate([noisy, cond], axis=1).astype(BF16))
        inp[...] = made[-1]
        tgt[...] = data - noise
    hidden = [dot(both, w[...]) for both in made]
    scales = [lax.rsqrt(jnp.mean(h * h, axis=1, keepdims=True) + EPS) for h in hidden]
    weights = jnp.concatenate([wqkv[0], wqkv[1], wqkv[2]], axis=1)
    outs = [dot((h * scale * gain[...]).astype(BF16), weights) for h, scale in zip(hidden, scales)]
    return [
        (
            (out[:, 0:128].astype(BF16).astype(F32) * HEAD ** (-0.5)).astype(BF16),
            out[:, 128:256].astype(BF16),
            out[:, 256:].astype(BF16),
        )
        for out in outs
    ]


def piece_kernel(step, table, x, w, gain, wqkv, inp, tgt, qkv):
    (out,) = pieces_of(table, w, gain, wqkv, [(step, x, inp, tgt)])
    for j in range(3):
        qkv[:, j * 128 : (j + 1) * 128] = out[j]


def piece_rows(step):
    part = lax.rem(lax.axis_index("mp") + step, 4)
    return [(b * 32, pl.ds(pl.multiple_of(b * BLOCK + part * 32, 32), 32)) for b in range(8)]


def front_kernel(
    table, p0, p1, x2, x3, w, gain, wqkv, att, attt, q, k, v, probs_out, i2, i3, t2, t3, vt
):
    made = pieces_of(table, w, gain, wqkv, [(2, x2, i2, t2), (3, x3, i3, t3)])
    early = [[p[:, j * 128 : (j + 1) * 128] for j in range(3)] for p in (p0, p1)]
    for step, piece in enumerate(early + made):
        for r, at in piece_rows(step):
            for ref, rows in zip((q, k, v), piece):
                ref[at, :] = rows[r : r + 32]
    vt[...] = v[...].T

    def one(first, rows):
        at = pl.ds(first, rows)
        keys = [jnp.where(head_mask(rows, h), k[at, :], jnp.zeros((), BF16)) for h in range(2)]
        scores = [dot(key, q[at, :], NT) for key in keys]
        weights = [jnp.exp(s - jnp.max(s, axis=0, keepdims=True)) for s in scores]
        inverse = [1.0 / jnp.sum(a, axis=0, keepdims=True) for a in weights]
        probs = [a * b for a, b in zip(weights, inverse)]
        parts = [dot(vt[h * HEAD : (h + 1) * HEAD, at], probs[h].astype(BF16)) for h in range(2)]
        for h in range(2):
            probs_out[h, at, 0:rows] = probs[h]
            attt[h * HEAD : (h + 1) * HEAD, at] = parts[h].astype(BF16)

    each_utterance(table, one)
    att[...] = attt[...].T


def mid_kernel(i0, i1, i2, i3, t0, t1, t2, t3, w, gain, k, hidden, normed, tgt, kt):
    kt[...] = k[...].T
    for step, (inp, target) in enumerate(((i0, t0), (i1, t1), (i2, t2), (i3, t3))):
        h = dot(inp[...], w[...])
        scale = lax.rsqrt(jnp.mean(h * h, axis=1, keepdims=True) + EPS)
        n = (h * scale * gain[...]).astype(BF16)
        for r, at in piece_rows(step):
            hidden[at, :] = h[r : r + 32]
            normed[at, :] = n[r : r + 32]
            tgt[at, :] = target[r : r + 32, :]


def mix_kernel(hidden, a0, a3, proj, out):
    weights = jnp.concatenate([proj[0:128, :], proj[384:512, :]], axis=0)
    for i in range(4):
        rows = pl.ds(i * 256, 256)
        out[rows, :] = hidden[rows, :] + dot(jnp.concatenate([a0[rows, :], a3[rows, :]], axis=1), weights)


def back_kernel(
    table, attt, a1, a2, proj, hidden, normed, tgt, fgain, vel, q, kt, v, probs,
    keep, send, back1, dout, dqt, dk, dv, lhs,
):
    spans = utterances(table)
    def first(i):
        rows = pl.ds(i * 256, 256)
        groups = jnp.concatenate([a1[rows, :], a2[rows, :]], axis=1)
        wide = (hidden[rows, :] + dot(groups, proj[128:384, :])).astype(BF16).astype(F32)
        return wide, lax.rsqrt(jnp.mean(wide * wide, axis=1, keepdims=True) + EPS)

    def second(i, wide, rscale):
        rows = pl.ds(i * 256, 256)
        normalized = wide * rscale
        velocity = dot((normalized * fgain[...]).astype(BF16), vel[...])
        frame = i * 256 + lax.broadcasted_iota(jnp.int32, (256, 128), 0)
        error = jnp.where(masked_of(frame, spans), 2.0 * (velocity - tgt[rows, :]), 0.0)
        return normalized, rscale, error.astype(BF16)

    def third(i, normalized, rscale, error):
        rows = pl.ds(i * 256, 256)
        scaled = dot(error, vel[...], NT) * fgain[...]
        middle = jnp.mean(scaled * normalized, axis=1, keepdims=True)
        b1 = (rscale * (scaled - normalized * middle)).astype(BF16)
        back1[rows, :] = b1
        dout[rows, :] = dot(b1, proj[0:128, :], NT).astype(BF16)

    ones = [first(i) for i in range(4)]
    twos = [second(i, *ones[i]) for i in range(4)]
    for i in range(4):
        third(i, *twos[i])


    def one(first, rows):
        at = pl.ds(first, rows)
        qs, vs, ds = q[at, :], v[at, :], dout[at, :]
        zero = jnp.zeros((), BF16)
        ps = [probs[h, at, 0:rows] for h in range(2)]
        dps = [
            dot(jnp.where(head_mask(rows, h), vs, zero), ds, NT).astype(BF16).astype(F32) for h in range(2)
        ]
        dvs = [dot(p.astype(BF16), ds) for p in ps]
        inner = [jnp.sum(p * dp, axis=0, keepdims=True) for p, dp in zip(ps, dps)]
        dscores = [(p * (dp - s)).astype(BF16) for p, dp, s in zip(ps, dps, inner)]
        dks = [dot(d, qs) for d in dscores]
        for h in range(2):
            span = slice(h * HEAD, (h + 1) * HEAD)
            dqt[span, at] = (dot(kt[span, at], dscores[h]) * HEAD ** (-0.5)).astype(BF16)
        mask = head_mask(rows, 0)
        dk[at, :] = jnp.where(mask, dks[0], dks[1]).astype(BF16)
        dv[at, :] = jnp.where(mask, dvs[0], dvs[1]).astype(BF16)

    each_utterance(table, one)
    lhs[0:128, :] = dqt[...]
    lhs[128:256, :] = dk[...].T
    lhs[256:384, :] = dv[...].T
    mine = lax.axis_index("c") == 0
    for j in range(4):
        cols = slice(j * 256, (j + 1) * 256)
        top = dot(lhs[0:384, :], normed[:, cols])
        low = dot(attt[...], back1[:, cols])
        terms = jnp.concatenate([top.T, low.T], axis=1).reshape(8, 2, 16, 512)
        even, odd = terms[:, 0], terms[:, 1]
        keep[2 * j : 2 * j + 2] = jnp.where(mine, even, odd).reshape(2, 4, 16, 512)
        send[2 * j : 2 * j + 2] = jnp.where(mine, odd, even).reshape(2, 4, 16, 512).astype(BF16)


def pair_kernel(keep, got, own, s1, s2, s3):
    y = lax.axis_index("y")
    own[...] = keep[:, y] + got[:, y].astype(F32)
    for by, ref in ((1, s1), (2, s2), (3, s3)):
        to = lax.rem(y + by, 4)
        ref[...] = (keep[:, to] + got[:, to].astype(F32)).astype(BF16)


def line_kernel(own, r1, r2, r3, out):
    total = own[...] + r1[...].astype(F32) + r2[...].astype(F32) + r3[...].astype(F32)
    out[...] = total.astype(BF16)


def finish_kernel(count, parts, qkv, out):
    total = jnp.sum(parts[...].astype(F32), axis=0) / count[...]
    for j in range(3):
        qkv[j] = total[:, j * 128 : (j + 1) * 128]
    out[...] = total[:, 384:]


def shards(
    noise_blocks, data_blocks, destination, utt_blocks, span_start, span_size, timestep,
    in_weight, norm_gain, qkv_weight, out_proj, final_gain, vel_weight,
):
    here, c = device(), lax.axis_index("c")
    swap = [(0, 1), (1, 0)]

    def turned(a, by):
        return lax.ppermute(a, "mp", [(i, (i - by) % 4) for i in range(4)])

    spans = (utt_blocks, span_start, span_size)
    own = pl.pallas_call(
        share_kernel,
        out_shape=jax.ShapeDtypeStruct((8, SLOT, 128), BF16),
        in_specs=[hb()] * 5,
        out_specs=vm(),
        scratch_shapes=[SMEM((1, 4), jnp.int32)] * 3
        + [VMEM((2, 8, 3200), BF16), VMEM((8 * SLOT, 128), F32), pltpu.SemaphoreType.DMA((5,))],
        compiler_params=params(ALL),
        name="share",
    )(*spans, noise_blocks, data_blocks)
    other = lax.ppermute(own, "c", swap)
    bins = destination // 8
    packed = pl.pallas_call(
        pack_kernel,
        out_shape=jax.ShapeDtypeStruct((32, PAIR, 128), BF16),
        in_specs=[sm(), hb(), hb()],
        out_specs=hb(),
        scratch_shapes=[
            VMEM((2, 8, 8, 128), BF16), VMEM((32, 8, 128), F32), VMEM((32, 8, 128), BF16),
            pltpu.SemaphoreType.DMA((2,)), pltpu.SemaphoreType.DMA((17,)),
        ],
        compiler_params=params(8),
        name="pack",
    )(bins, own, other)
    packed, in_weight, qkv_weight, out_proj, vel_weight, norm_gain, final_gain, table = lax.optimization_barrier(
        (packed, in_weight, qkv_weight, out_proj, vel_weight, norm_gain, final_gain, spans + (timestep,))
    )
    table = jnp.concatenate(table, axis=1)
    w = jnp.concatenate(
        [jnp.pad(in_weight[:MEL], ((0, 28), (0, 0))), jnp.pad(in_weight[MEL:], ((0, 28), (0, 0)))], axis=0
    )
    gain = norm_gain.astype(F32)[None, :]
    fgain = final_gain.astype(F32)[None, :]
    wqkv = qkv_weight.transpose(1, 0, 2)
    vel = jnp.pad(vel_weight, ((0, 0), (0, 28)))
    proj = jnp.concatenate([out_proj] + [turned(out_proj, by) for by in (1, 2, 3)], axis=0)
    arrived = lax.all_to_all(packed, ("z", "y"), 0, 0, tiled=True)
    wanted = here * 8 + jnp.arange(8, dtype=jnp.int32)
    row = jnp.sum(
        jnp.where(destination[None, :] == wanted[:, None], jnp.arange(512, dtype=jnp.int32)[None, :], 0), axis=1
    )
    source = (row >> 4) * 2 + (((row >> 3) & 1) ^ c)
    arrived, source, w, gain, fgain, wqkv, vel, proj, table = lax.optimization_barrier(
        (arrived, source, w, gain, fgain, wqkv, vel, proj, table)
    )
    frames = pl.pallas_call(
        unpack_kernel,
        out_shape=jax.ShapeDtypeStruct((256, 256), BF16),
        in_specs=[sm(), hb()],
        out_specs=vm(),
        scratch_shapes=[
            VMEM((8, 48, 128), BF16), VMEM((8, 8, 128), BF16), VMEM((8 * SLOT, 128), F32),
            VMEM((256, 128), F32), pltpu.SemaphoreType.DMA((16,)),
        ],
        compiler_params=params(8),
        name="unpack",
    )(source, arrived)
    counts = jnp.sum(arrived[:, 100:102, 0:2].astype(F32), axis=(0, 1))
    count = counts[0] * 32.0 + counts[1]
    pieces = [frames] + [turned(frames, by) for by in (1, 2, 3)]

    half, turn = (jax.ShapeDtypeStruct(shape, BF16) for shape in ((1024, 128), (128, 1024)))

    def cost(flops, size):
        return pl.CostEstimate(flops=flops, bytes_accessed=size, transcendentals=0)

    def piece(step, frames):
        return pl.pallas_call(
            functools.partial(piece_kernel, step),
            out_shape=(
                jax.ShapeDtypeStruct((256, 256), BF16), jax.ShapeDtypeStruct((256, 128), F32),
                jax.ShapeDtypeStruct((256, 384), BF16),
            ),
            in_specs=[sm()] + [vm()] * 4,
            out_specs=(vm(),) * 3,
            compiler_params=params(12),
            cost_estimate=cost(1 << 29, 2 << 20),
            name=f"piece{step}",
        )(table, frames, w, gain, wqkv)

    first = [piece(step, pieces[step]) for step in (0, 1)]
    att, attt, q, k, v, probs, *late = pl.pallas_call(
        front_kernel,
        out_shape=(half, turn, half, half, half, jax.ShapeDtypeStruct((2, 1024, 512), F32))
        + (jax.ShapeDtypeStruct((256, 256), BF16),) * 2 + (jax.ShapeDtypeStruct((256, 128), F32),) * 2,
        in_specs=[sm()] + [vm()] * 7,
        out_specs=(vm(),) * 10,
        scratch_shapes=[VMEM((128, 1024), BF16)],
        compiler_params=params(20),
        name="front",
    )(table, first[0][2], first[1][2], pieces[2], pieces[3], w, gain, wqkv)
    inp = (first[0][0], first[1][0], late[0], late[1])
    tgt = (first[0][1], first[1][1], late[2], late[3])
    heads = [att] + [turned(att, by) for by in (1, 2, 3)]
    full = jax.ShapeDtypeStruct((1024, 1024), F32)
    hidden, normed, target, kt = pl.pallas_call(
        mid_kernel,
        out_shape=(full, jax.ShapeDtypeStruct((1024, 1024), BF16), jax.ShapeDtypeStruct((1024, 128), F32), turn),
        in_specs=[vm()] * 11,
        out_specs=(vm(),) * 4,
        compiler_params=params(14),
        cost_estimate=cost(1 << 29, 7 << 20),
        name="mid",
    )(*inp, *tgt, w, gain, k)
    hidden = pl.pallas_call(
        mix_kernel,
        out_shape=full,
        in_specs=[vm()] * 4,
        out_specs=vm(),
        input_output_aliases={0: 0},
        compiler_params=params(14),
        cost_estimate=cost(1 << 29, 7 << 20),
        name="mix",
    )(hidden, heads[0], heads[3], proj)
    keep, send = pl.pallas_call(
        back_kernel,
        out_shape=tuple(jax.ShapeDtypeStruct((8, 4, 16, 512), t) for t in (F32, BF16)),
        in_specs=[sm()] + [vm()] * 13,
        out_specs=(vm(), vm()),
        scratch_shapes=[
            VMEM((1024, 1024), BF16), VMEM((1024, 128), BF16),
            VMEM((128, 1024), BF16), VMEM((1024, 128), BF16), VMEM((1024, 128), BF16),
            VMEM((384, 1024), BF16),
        ],
        compiler_params=params(28),
        name="back",
    )(table, attt, *heads[1:3], proj, hidden, normed, target, fgain, vel, q, kt, v, probs)
    got = lax.ppermute(send, "c", swap)
    piece = jax.ShapeDtypeStruct((8, 16, 512), BF16)
    total, *sends = pl.pallas_call(
        pair_kernel,
        out_shape=(jax.ShapeDtypeStruct((8, 16, 512), F32), piece, piece, piece),
        in_specs=[vm()] * 2,
        out_specs=(vm(),) * 4,
        compiler_params=params(8),
        name="pair",
    )(keep, got)
    others = [
        lax.ppermute(a, "y", [(i, (i + by) % 4) for i in range(4)]) for by, a in zip((1, 2, 3), sends)
    ]
    line = pl.pallas_call(
        line_kernel,
        out_shape=piece,
        in_specs=[vm()] * 4,
        out_specs=vm(),
        compiler_params=params(8),
        name="line",
    )(total, *others)
    parts = lax.all_to_all(line, "z", 0, 0, tiled=True)
    grad_qkv, grad_out = pl.pallas_call(
        finish_kernel,
        out_shape=(jax.ShapeDtypeStruct((3, 16, 128), F32), jax.ShapeDtypeStruct((16, 128), F32)),
        in_specs=[vm()] * 2,
        out_specs=(vm(), vm()),
        compiler_params=params(8),
        name="finish",
    )(count.reshape(1, 1), parts)
    return (grad_qkv.transpose(1, 0, 2), grad_out.T)


def solution(mesh):
    dp = ("z", "y", "c")
    fine = Mesh(mesh.devices.reshape(8, 4, 2, 4), dp + ("mp",))
    row = P(dp, None)
    in_specs = (
        row, row, P(), row, row, row, row, P(), P(), P(None, None, "mp"), P("mp", None), P(), P(),
    )
    out_specs = (P(dp, None, "mp"), P("mp", dp))
    return jax.shard_map(shards, mesh=fine, in_specs=in_specs, out_specs=out_specs, check_vma=False)
```
